128 devices in a mesh: grp: 2 (over z_hi), wid: 8 (over y, core), hid: 8 (over z_lo, x).
Axes of the slice: x: 4, y: 4, z: 4 (z_hi: 2, z_lo: 2; z = z_hi * 2 + z_lo), core: 2. Of those that a mesh axis runs over, the one named last changes fastest.
Arguments:
- student_in: bfloat16 [1024, 4096], P('wid'), may hold values from -6 to 6
- norm_gain: float32 [4096], replicated, may hold values from 0.1 to 1.9
- gate_weight: bfloat16 [4096, 7168], P(None, ('grp', 'hid')), may hold values from -0.09375 to 0.09375
- up_weight: bfloat16 [4096, 7168], P(None, ('grp', 'hid')), may hold values from -0.09375 to 0.09375
- down_weight: bfloat16 [7168, 4096], P(('grp', 'hid')), may hold values from -0.0625 to 0.0625
- projection: bfloat16 [4096, 8, 1024], P(None, None, ('grp', 'hid')), may hold values from -0.09375 to 0.09375
- teacher_in: bfloat16 [1024, 8192], P(None, 'wid'), may hold values from -6 to 6
- teacher_gate: bfloat16 [8192, 14336], P('wid', ('grp', 'hid')), may hold values from -0.0625 to 0.0625
- teacher_up: bfloat16 [8192, 14336], P('wid', ('grp', 'hid')), may hold values from -0.0625 to 0.0625
- teacher_down: bfloat16 [14336, 8192], P(('grp', 'hid'), 'wid'), may hold values from -0.046875 to 0.046875
Outputs:
- grad_gate: bfloat16 [4096, 7168], P('wid', ('grp', 'hid'))
- grad_up: bfloat16 [4096, 7168], P('wid', ('grp', 'hid'))
- grad_down: bfloat16 [7168, 4096], P(('grp', 'hid'), 'wid')
- grad_proj: bfloat16 [4096, 8, 1024], P('wid', None, ('grp', 'hid'))
- input_grad: float32 [1024, 4096], P('wid', ('grp', 'hid'))
The draws below stay inside these ranges and needn't reach their ends.
All inputs are finite; a program needn't handle non-finite values.
Results may differ from the reference program's by a relative error of at most 0.02.
Values may be sent and summed in bfloat16 or wider, within the bound.
A program may use at most 128 MiB of HBM per device.

```python
import math
import jax
import jax.numpy as jnp
from jax import lax

D_T = 8192
FF_T = 14336
D_S = 4096
FF_S = 7168
TOKENS = 1024
TW = 1024
N_WID = 8


def block_levels(own_key, extent, shards, least, high):
    loudness = 1.0
    for position, shards_of in shards:
        steps = jax.random.uniform(jax.random.fold_in(jax.random.fold_in(own_key, 6), position), (shards_of,), jnp.float32, least / len(shards), high / len(shards))
        loudness = loudness * jnp.repeat(jnp.exp(steps), extent[position] // shards_of).reshape((-1,) + (1,) * (len(extent) - 1 - position))
    return loudness


def gaussian(rng, extent, width, limit, cuts=(), kind=jnp.bfloat16):
    drawn = width * jax.random.normal(rng, extent, jnp.float32)
    if cuts:
        drawn = drawn * block_levels(rng, extent, cuts, -0.22, 0.18)
    return jnp.clip(drawn, -limit, limit).astype(kind)


def setup_inputs(seed: int = 0) -> dict:
    splits = jax.random.split(jax.random.key(seed), 11)
    return {
        "student_in": gaussian(splits[0], (TOKENS, D_S), 1.0, 6.0, ((0, 8),)),
        "norm_gain": jnp.clip(1.0 + 0.18 * jax.random.normal(splits[1], (D_S,), jnp.float32), 0.1, 1.9),
        "gate_weight": gaussian(splits[2], (D_S, FF_S), D_S ** -0.5, 0.09375, ((1, 16),)),
        "up_weight": gaussian(splits[3], (D_S, FF_S), D_S ** -0.5, 0.09375, ((1, 16),)),
        "down_weight": gaussian(splits[4], (FF_S, D_S), FF_S ** -0.5, 0.0625, ((0, 16),)),
        "projection": gaussian(splits[5], (D_S, N_WID, TW), D_S ** -0.5, 0.09375, ((2, 16),)),
        "teacher_in": gaussian(splits[6], (TOKENS, D_T), 1.0, 6.0, ((1, 8),)),
        "teacher_gate": gaussian(splits[7], (D_T, FF_T), D_T ** -0.5, 0.0625, ((0, 8), (1, 16))),
        "teacher_up": gaussian(splits[8], (D_T, FF_T), D_T ** -0.5, 0.0625, ((0, 8), (1, 16))),
        "teacher_down": gaussian(splits[9], (FF_T, D_T), FF_T ** -0.5, 0.046875, ((0, 16), (1, 8))),
    }


def reference(student_in, norm_gain, gate_weight, up_weight, down_weight, projection, teacher_in, teacher_gate, teacher_up, teacher_down):
    f32 = jnp.float32
    bf16 = jnp.bfloat16
    teacher_gate_sum = jnp.dot(teacher_in, teacher_gate, preferred_element_type=f32)
    teacher_up_sum = jnp.dot(teacher_in, teacher_up, preferred_element_type=f32)
    teacher_hidden = (teacher_gate_sum * jax.nn.sigmoid(teacher_gate_sum) * teacher_up_sum).astype(bf16)
    target = jnp.dot(teacher_hidden, teacher_down, preferred_element_type=f32).astype(bf16)
    inputs = student_in.astype(f32)
    inverse_rms = lax.rsqrt(lax.optimization_barrier(jnp.mean(inputs * inputs, axis=-1, keepdims=True)) + 1e-05)
    normed = (inputs * inverse_rms * norm_gain).astype(bf16)
    gate = jnp.dot(normed, gate_weight, preferred_element_type=f32)
    up_sum = jnp.dot(normed, up_weight, preferred_element_type=f32)
    sigma = jax.nn.sigmoid(gate)
    hidden = (gate * sigma * up_sum).astype(bf16)
    branch = jnp.dot(hidden, down_weight, preferred_element_type=f32)
    summed = (inputs + branch).astype(bf16)
    proj_matrix = projection.reshape(D_S, D_T)
    features = jnp.dot(summed, proj_matrix, preferred_element_type=f32)
    feature_error = ((features - target.astype(f32)) / math.sqrt(TOKENS)).astype(bf16)
    feature_grad = jnp.dot(feature_error, proj_matrix.T, preferred_element_type=f32)
    branch_grad = feature_grad.astype(bf16)
    hidden_grad = jnp.dot(branch_grad, down_weight.T, preferred_element_type=f32)
    gate_grad = (hidden_grad * up_sum * sigma * (1.0 + gate * (1.0 - sigma))).astype(bf16)
    up_grad = (hidden_grad * gate * sigma).astype(bf16)
    normed_grad = jnp.dot(gate_grad, gate_weight.T, preferred_element_type=f32) + jnp.dot(up_grad, up_weight.T, preferred_element_type=f32)
    scaled = normed_grad * norm_gain
    moment = lax.optimization_barrier(jnp.mean(scaled * inputs, axis=-1, keepdims=True))
    input_grad = feature_grad + inverse_rms * (scaled - inputs * inverse_rms * inverse_rms * moment)
    grad_gate = jnp.dot(normed.T, gate_grad, preferred_element_type=f32).astype(bf16)
    grad_up = jnp.dot(normed.T, up_grad, preferred_element_type=f32).astype(bf16)
    grad_down = jnp.dot(hidden.T, branch_grad, preferred_element_type=f32).astype(bf16)
    grad_proj = jnp.dot(summed.T, feature_error, preferred_element_type=f32).astype(bf16).reshape(D_S, N_WID, TW)
    return (grad_gate, grad_up, grad_down, grad_proj, input_grad)
```

```python
import jax
import jax.numpy as jnp
from jax import lax
from jax.experimental import pallas as pl
from jax.experimental.pallas import tpu as pltpu
from jax.sharding import Mesh
from jax.sharding import PartitionSpec as P

MESH = pl.DeviceIdType.MESH
F32 = jnp.float32
BF16 = jnp.bfloat16
WID = ("y", "c")
GH = ("zh", "zl", "x")
SEMS = 320

NN = (((1,), (0,)), ((), ()))
NT = (((1,), (1,)), ((), ()))
TN = (((0,), (0,)), ((), ()))


def mm(a, b, dims):
    return lax.dot_general(a, b, dims, preferred_element_type=F32)


def up(v):
    return v.astype(F32)


def mod4(v):
    return lax.rem(v, 4)


class Net:
    def __init__(self, send, recv):
        zh, y, c, zl, x = [lax.axis_index(a) for a in ("zh", "y", "c", "zl", "x")]
        self.z, self.x, self.y, self.c = zh * 2 + zl, x, y, c
        self.send, self.recv, self.copies = send, recv, []

    def at(self, z=None, x=None, y=None, c=None):
        z = self.z if z is None else z
        return {
            "zh": lax.div(z, 2),
            "zl": lax.rem(z, 2),
            "x": self.x if x is None else x,
            "y": self.y if y is None else y,
            "c": self.c if c is None else c,
        }

    def along(self, axis, offset):
        return self.at(**{axis: mod4(getattr(self, axis) + offset)})

    def put(self, src, dst, peer):
        i = len(self.copies)
        copy = pltpu.make_async_remote_copy(
            src_ref=src,
            dst_ref=dst,
            send_sem=self.send.at[i],
            recv_sem=self.recv.at[i],
            device_id=peer,
            device_id_type=MESH,
        )
        copy.start()
        self.copies.append(copy)
        return copy


class RingSum:
    def __init__(self, net, axis, src, buf):
        self.net, self.axis, self.src, self.buf = net, axis, src, buf
        me = getattr(net, axis)
        self.me, self.r, self.o, self.l = me, mod4(me + 1), mod4(me + 2), mod4(me + 3)
        self.right, self.left = net.along(axis, 1), net.along(axis, 3)

    def far(self):
        self.m1 = self.net.put(self.src(self.o, 0), self.buf.at[0], self.right)
        self.n1 = self.net.put(self.src(self.o, 1), self.buf.at[1], self.left)

    def near_r(self):
        self.m2 = self.net.put(self.src(self.r, 1), self.buf.at[2], self.right)

    def near_l(self):
        self.n2 = self.net.put(self.src(self.l, 0), self.buf.at[3], self.left)

    def start(self):
        self.far()
        self.near_r()
        self.near_l()

    def relay(self):
        buf = self.buf
        self.m1.wait_recv()
        buf[0] = (up(buf[0]) + up(self.src(self.r, 0)[...])).astype(BF16)
        self.m3 = self.net.put(buf.at[0], buf.at[4], self.right)
        self.n1.wait_recv()
        buf[1] = (up(buf[1]) + up(self.src(self.l, 1)[...])).astype(BF16)
        self.n3 = self.net.put(buf.at[1], buf.at[5], self.left)

    def finish(self):
        buf = self.buf
        self.n2.wait_recv()
        self.m3.wait_recv()
        first = up(self.src(self.me, 0)[...]) + up(buf[3]) + up(buf[4])
        self.m2.wait_recv()
        self.n3.wait_recv()
        second = up(self.src(self.me, 1)[...]) + up(buf[2]) + up(buf[5])
        return first, second


class PlaneSum:
    def __init__(self, net, j, data, q, buf1, mid, buf2):
        self.net, self.mid = net, mid
        if j == 0:
            src, axes = (lambda d, h: data.at[:, d, q[h]]), ("x", "z")
        else:
            src, axes = (lambda d, h: data.at[d, :, q[h]]), ("z", "x")
        self.one = RingSum(net, axes[0], src, buf1)
        self.two = RingSum(net, axes[1], lambda d, h: mid.at[h, d], buf2)

    def start(self):
        self.one.start()

    def relay1(self):
        self.one.relay()

    def turn(self):
        first, second = self.one.finish()
        self.mid[0] = first.astype(BF16)
        self.mid[1] = second.astype(BF16)
        self.two.start()

    def relay2(self):
        self.two.relay()

    def finish(self):
        return self.two.finish()


class RingAll:
    def __init__(self, net, axis, whole, part):
        self.net, self.whole, self.part = net, whole, part
        me = getattr(net, axis)
        self.me, self.r, self.l = me, mod4(me + 1), mod4(me + 3)
        self.right, self.left = net.along(axis, 1), net.along(axis, 3)

    def start(self):
        own = self.whole(self.me)
        self.m1 = self.net.put(own, own, self.right)
        self.n1 = self.net.put(own, own, self.left)

    def relay(self):
        self.m1.wait_recv()
        piece = self.part(self.l, 0)
        self.m2 = self.net.put(piece, piece, self.right)
        self.n1.wait_recv()
        piece = self.part(self.r, 1)
        self.n2 = self.net.put(piece, piece, self.left)

    def finish(self):
        self.m2.wait_recv()
        self.n2.wait_recv()


class PlaneAll:
    def __init__(self, net, data):
        z, x = net.z, net.x
        self.a1 = RingAll(
            net, "z", lambda d: data.at[d, x, pl.ds(0, 2)], lambda d, h: data.at[d, x, h]
        )
        self.b1 = RingAll(
            net, "x", lambda d: data.at[z, d, pl.ds(2, 2)], lambda d, h: data.at[z, d, 2 + h]
        )
        self.a2 = RingAll(
            net, "x", lambda d: data.at[:, d, pl.ds(0, 2)], lambda d, h: data.at[:, d, h]
        )
        self.b2 = RingAll(
            net, "z", lambda d: data.at[d, :, pl.ds(2, 2)], lambda d, h: data.at[d, :, 2 + h]
        )

    def start(self):
        self.a1.start()
        self.b1.start()

    def relay1(self):
        self.a1.relay()
        self.b1.relay()

    def turn(self):
        self.a1.finish()
        self.a2.start()
        self.b1.finish()
        self.b2.start()

    def relay2(self):
        self.a2.relay()
        self.b2.relay()

    def finish(self):
        self.a2.finish()
        self.b2.finish()


class TokenAll:
    def __init__(self, net, data):
        rows = data.shape[0]
        self.net, self.data = net, data

        def slot(d, c, h=None):
            at = pl.multiple_of((d * 2 + c) * 128, 128)
            if h is None:
                return data.at[:, pl.ds(at, 128)]
            return data.at[pl.ds(h * (rows // 2), rows // 2), pl.ds(at, 128)]

        self.slot = slot
        self.ring = RingAll(
            net, "y", lambda d: slot(d, net.c), lambda d, h: slot(d, net.c, h)
        )
        self.own = slot(net.y, net.c)
        self.mate = net.at(c=1 - net.c)
        self.mates = {}

    def share(self, offset):
        piece = self.slot(mod4(self.net.y + offset), self.net.c)
        self.mates[offset] = self.net.put(piece, piece, self.mate)

    def start(self):
        self.ring.start()
        self.share(0)

    def relay(self):
        self.ring.relay()
        self.share(1)
        self.share(3)

    def finish(self):
        self.ring.finish()
        self.share(2)

    def wait(self, offset):
        self.mates[offset].wait_recv()


class Columns:
    def __init__(self, net, source, data):
        self.net, self.source, self.data = net, source, data
        self.plane = PlaneAll(net, data)

    def spread(self):
        net = self.net
        rows = pl.ds(pl.multiple_of(lax.div(net.x, 2) * 16, 16), 16)
        half = lax.rem(net.x, 2)
        to = self.data.at[net.z, net.x, net.y, pl.ds(pl.multiple_of(net.c * 16, 16), 16)]

        def piece(y, c):
            return self.source.at[y, 2 * c + half, net.z, rows]

        to[...] = piece(net.y, net.c)[...]
        self.copies = []
        for offset in (2, 1, 3, 0):
            for flip in (0, 1):
                if offset or flip:
                    y, c = mod4(net.y + offset), lax.rem(net.c + flip, 2)
                    self.copies.append(net.put(piece(y, c), to, net.at(y=y, c=c)))

    def start(self):
        for copy in self.copies:
            copy.wait_recv()
        self.plane.start()

    def unpack(self, out):
        data = self.data

        def body(y, _):
            for c in (0, 1):
                for half in (0, 1):
                    parts = [
                        data[z, 2 * i + half, y, 16 * c : 16 * c + 16]
                        for z in range(4)
                        for i in (0, 1)
                    ]
                    at = pl.multiple_of(y * 256 + c * 128, 128)
                    out[pl.ds(at, 128), 256 * half : 256 * half + 256] = jnp.concatenate(
                        parts, axis=0
                    )
            return 0

        lax.fori_loop(0, 4, body, 0)


def share_of(ref, z, x):
    return ref[z, x].reshape(128, 256)


def wide_of(ref, z):
    return jnp.concatenate([share_of(ref, z, x) for x in range(4)], axis=1)


def kernel(
    student_in,
    norm_gain,
    gate_weight,
    up_weight,
    down_weight,
    projection,
    teacher_in,
    teacher_gate,
    teacher_up,
    teacher_down,
    grad_gate,
    grad_up,
    grad_down,
    grad_proj,
    input_grad,
    xin,
    gain,
    wg,
    wu,
    wd,
    pj,
    tin,
    tg,
    tu,
    td,
    tdt,
    parts,
    mate,
    ring,
    thid,
    feat,
    feat1,
    featm,
    feat2,
    sums,
    sums1,
    summ,
    sums2,
    normed,
    summed,
    bgrad,
    ncols,
    scols,
    bcols,
    flat,
    hids,
    errs,
    ggs,
    gate,
    upsum,
    sigma,
    acc,
    acc2,
    tshare,
    target,
    fgrad,
    stat,
    statx,
    statz,
    invs,
    load,
    send,
    recv,
):
    net = Net(send, recv)
    z, x, y, c = net.z, net.x, net.y, net.c
    ys = [mod4(y + o) for o in range(4)]

    loads = {}
    for i, (name, src, dst) in enumerate(
        (
            ("xin", student_in, xin),
            ("gain", norm_gain, gain),
            ("tin", teacher_in, tin),
            ("tg", teacher_gate, tg),
            ("tu", teacher_up, tu),
            ("wg", gate_weight, wg),
            ("wu", up_weight, wu),
            ("wd", down_weight, wd),
            ("td", teacher_down, td),
            ("pj", projection, pj),
        )
    ):
        loads[name] = pltpu.make_async_copy(src, dst, load.at[i])
        loads[name].start()

    barrier = pltpu.get_barrier_semaphore()
    peers = [net.at(y=mod4(y + o), c=lax.rem(c + f, 2)) for o in range(4) for f in (0, 1) if o or f]
    peers += [net.along("x", o) for o in (1, 2, 3)] + [net.along("z", o) for o in (1, 2, 3)]
    for peer in peers:
        pl.semaphore_signal(barrier, inc=1, device_id=peer, device_id_type=MESH)

    loads["xin"].wait()
    loads["gain"].wait()

    def squares(b, total):
        v = up(xin[:, pl.ds(pl.multiple_of(b * 256, 256), 256)])
        return total + v * v

    total = lax.fori_loop(0, 16, squares, jnp.zeros((128, 256), F32))
    inv = lax.rsqrt(jnp.sum(total, axis=1, keepdims=True) / 4096.0 + 1e-05)
    invs[...] = jnp.broadcast_to(inv, (128, 128))

    def norm(b, _):
        at = pl.ds(pl.multiple_of(b * 256, 256), 256)
        scale = jnp.concatenate([invs[...], invs[...]], axis=1)
        v = up(xin[:, at]) * scale * gain[:, at]
        normed[lax.div(b, 4), lax.rem(b, 4)] = v.astype(BF16).reshape(4, 32, 256)
        return 0

    lax.fori_loop(0, 16, norm, 0)
    pl.semaphore_wait(barrier, len(peers))
    ncol = Columns(net, normed, ncols)
    ncol.spread()

    tsum = RingSum(
        net, "y", lambda d, h: parts.at[d, c, pl.ds(64 * h, 64)], ring
    )
    for name in ("tin", "tg", "tu"):
        loads[name].wait()
    pair = {}

    def project(o):
        d = ys[o]
        rows = tin[pl.ds(pl.multiple_of(d * 256, 256), 256), :]
        parts[d, :, :, 0:896] = mm(rows, tg[...], NN).astype(BF16).reshape(2, 128, 896)
        parts[d, :, :, 896:1792] = mm(rows, tu[...], NN).astype(BF16).reshape(2, 128, 896)

    def swap(o):
        d = ys[o]
        pair[o] = net.put(parts.at[d, 1 - c], mate.at[d], net.at(c=1 - c))

    def join(o):
        d = ys[o]
        pair[o].wait_recv()
        parts[d, c] = (up(parts[d, c]) + up(mate[d])).astype(BF16)

    project(2)
    swap(2)
    ncol.start()
    project(1)
    swap(1)
    join(2)
    tsum.far()
    ncol.plane.relay1()
    project(3)
    swap(3)
    join(1)
    tsum.near_r()
    ncol.plane.turn()
    project(0)
    swap(0)
    join(3)
    tsum.near_l()
    ncol.plane.relay2()

    for name in ("wg", "wu", "wd"):
        loads[name].wait()

    def students(first, second, source, out_first, out_second):
        def body(b, _):
            at = pl.ds(pl.multiple_of(b * 1024, 1024), 1024)
            wide = wide_of(source, b)
            out_first[...] += mm(first[:, at], wide, NT)
            if second is not None:
                out_second[...] += mm(second[:, at], wide, NT)
            return 0

        out_first[...] = jnp.zeros(out_first.shape, F32)
        if second is not None:
            out_second[...] = jnp.zeros(out_second.shape, F32)
        lax.fori_loop(0, 4, body, 0)

    def back(out, pairs):
        def body(b, _):
            at = pl.ds(pl.multiple_of(b * 1024, 1024), 1024)
            v = sum(mm(small, w[:, at], TN) for small, w in pairs).astype(BF16)
            for i in range(4):
                out[b, i] = v[:, 256 * i : 256 * i + 256].reshape(4, 32, 256)
            return 0

        lax.fori_loop(0, 4, body, 0)

    students(wg, wu, normed, gate, upsum)
    tsum.relay()
    sig = jax.nn.sigmoid(gate[...])
    sigma[...] = sig
    hid = (gate[...] * sig * upsum[...]).astype(BF16)
    hiddens = TokenAll(net, hids)
    hiddens.own[...] = hid

    def plane_sums(n):
        return [
            PlaneSum(
                net, j, sums.at[n], (2 * j, 2 * j + 1), sums1.at[n, j], summ.at[n, j], sums2.at[n, j]
            )
            for j in (0, 1)
        ]

    back(sums.at[0], ((hid, wd),))
    branch = plane_sums(0)
    for s in branch:
        s.start()

    loads["td"].wait()
    tdt[...] = td[...].T
    join(0)
    ncol.plane.finish()
    for s in branch:
        s.relay1()

    first, second = tsum.finish()
    sums_all = jnp.concatenate([first, second], axis=0)
    g = sums_all[:, :896]
    teach = g * jax.nn.sigmoid(g) * sums_all[:, 896:]
    teachers = TokenAll(net, thid)
    teachers.own[...] = teach.T.astype(BF16)
    teachers.start()
    for s in branch:
        s.turn()

    order = [ys[0], ys[1], ys[3], ys[2]]

    def feature(o):
        d = ys[o]
        teachers.wait(o)
        v = mm(tdt[...], thid[:, pl.ds(pl.multiple_of(d * 256, 256), 256)], NN).astype(BF16)
        for f in (0, 1):
            feat[:, :, d, 64 * f : 64 * f + 64] = v[:, 128 * f : 128 * f + 128].reshape(
                4, 4, 64, 128
            )

    teaching = [
        PlaneSum(net, j, feat, (order[2 * j], order[2 * j + 1]), feat1.at[j], featm.at[j], feat2.at[j])
        for j in (0, 1)
    ]
    feature(0)
    for s in branch:
        s.relay2()
    teachers.relay()
    feature(1)
    teaching[0].start()

    rows_of = lambda q: pl.ds(32 * q, 32)
    share_at = pl.ds(pl.multiple_of((z * 4 + x) * 256, 256), 256)
    for j in (0, 1):
        for h, v in enumerate(branch[j].finish()):
            q = 2 * j + h
            summed[z, x, q] = (up(xin[rows_of(q), share_at]) + v).astype(BF16)
    sum_all = PlaneAll(net, summed)
    sum_all.start()
    feature(3)
    teachers.finish()
    sum_all.relay1()
    teaching[0].relay1()
    feature(2)
    teaching[1].start()
    hiddens.start()
    sum_all.turn()
    teaching[0].turn()
    teaching[1].relay1()
    sum_all.relay2()
    teaching[0].relay2()
    teaching[1].turn()
    hiddens.relay()
    sum_all.finish()
    scol = Columns(net, summed, scols)
    scol.spread()
    loads["pj"].wait()
    students(pj, None, summed, acc, None)

    sent = []

    def hand(k, v):
        d = order[k]
        tshare[d] = v.astype(BF16)
        to = target.at[pl.ds(pl.multiple_of((y * 2 + c) * 64, 64), 64)]
        for f in (0, 1):
            cc = lax.rem(c + f, 2)
            piece = tshare.at[d, pl.ds(pl.multiple_of(cc * 64, 64), 64)]
            if k == 0 and f == 0:
                to[...] = piece[...]
            else:
                sent.append(net.put(piece, to, net.at(y=d, c=cc)))

    for k, v in enumerate(teaching[0].finish()):
        hand(k, v)
    teaching[1].relay2()
    for k, v in enumerate(teaching[1].finish()):
        hand(2 + k, v)
    scol.start()
    hiddens.finish()
    scol.plane.relay1()
    for copy in sent:
        copy.wait_recv()

    err = ((acc[...] - up(target[...])) * (1.0 / 32.0)).astype(BF16)
    errors = TokenAll(net, errs)
    errors.own[...] = err
    errors.start()
    back(sums.at[1], ((err, pj),))
    grads = plane_sums(1)
    for s in grads:
        s.start()
    scol.plane.turn()
    for s in grads:
        s.relay1()
    errors.relay()
    scol.plane.relay2()
    for s in grads:
        s.turn()
    errors.finish()
    for o in (1, 3, 2):
        hiddens.wait(o)
    hiddens.wait(0)
    for s in grads:
        s.relay2()
    for j in (0, 1):
        for h, v in enumerate(grads[j].finish()):
            q = 2 * j + h
            fgrad[rows_of(q), :] = v
            bgrad[z, x, q] = v.astype(BF16)
    grad_all = PlaneAll(net, bgrad)
    grad_all.start()
    scol.plane.finish()
    scol.unpack(flat)
    grad_all.relay1()
    for o in range(4):
        errors.wait(o)
    grad_proj[0:256] = mm(errs[0:256], flat[...], NN).astype(BF16)
    grad_all.turn()
    grad_proj[256:512] = mm(errs[256:512], flat[...], NN).astype(BF16)
    ncol.unpack(flat)
    grad_all.relay2()
    grad_all.finish()
    bcol = Columns(net, bgrad, bcols)
    bcol.spread()

    students(wd, None, bgrad, acc2, None)
    hg = acc2[...]
    g, s = gate[...], sigma[...]
    gg = (hg * upsum[...] * s * (1.0 + g * (1.0 - s))).astype(BF16)
    ug = (hg * g * s).astype(BF16)
    moment = jnp.sum(up(gg) * g + up(ug) * upsum[...], axis=0, keepdims=True)
    gates = TokenAll(net, ggs)
    ggs[0:448, pl.ds(pl.multiple_of((y * 2 + c) * 128, 128), 128)] = gg
    ggs[448:896, pl.ds(pl.multiple_of((y * 2 + c) * 128, 128), 128)] = ug
    gates.start()
    statx[x] = jnp.broadcast_to(moment, (8, 128))
    stats = [net.put(statx.at[x], statx.at[x], net.along("x", o)) for o in (1, 2, 3)]
    back(sums.at[2], ((gg, wg), (ug, wu)))
    inner = plane_sums(2)
    for s in inner:
        s.start()
    for copy in stats:
        copy.wait_recv()
    statz[z] = statx[0] + statx[1] + statx[2] + statx[3]
    stats = [net.put(statz.at[z], statz.at[z], net.along("z", o)) for o in (1, 2, 3)]
    bcol.start()
    for s in inner:
        s.relay1()
    bcol.plane.relay1()
    for s in inner:
        s.turn()
    gates.relay()
    bcol.plane.turn()
    for copy in stats:
        copy.wait_recv()
    whole = (statz[0] + statz[1] + statz[2] + statz[3]) / 4096.0
    stat[...] = jnp.broadcast_to(whole[0:1], (128, 128)).T
    for s in inner:
        s.relay2()
    gates.finish()
    bcol.plane.relay2()
    for j in (0, 1):
        for h, v in enumerate(inner[j].finish()):
            r = rows_of(2 * j + h)
            scale = jnp.concatenate([invs[r, :], invs[r, :]], axis=1)
            mean = jnp.concatenate([stat[r, :], stat[r, :]], axis=1)
            scaled = v * gain[:, share_at]
            input_grad[r, :] = fgrad[r, :] + scale * (
                scaled - up(xin[r, share_at]) * scale * mean
            )
    for o in range(4):
        gates.wait(o)
    grad_gate[...] = mm(ggs[0:448], flat[...], NN).astype(BF16)
    grad_up[...] = mm(ggs[448:896], flat[...], NN).astype(BF16)
    bcol.plane.finish()
    bcol.unpack(flat)
    grad_down[...] = mm(hids[...], flat[...], NN).astype(BF16)
    for copy in net.copies:
        copy.wait_send()


def shards(
    student_in,
    norm_gain,
    gate_weight,
    up_weight,
    down_weight,
    projection,
    teacher_in,
    teacher_gate,
    teacher_up,
    teacher_down,
):
    vmem = pltpu.VMEM
    anyspec = pl.BlockSpec(memory_space=pl.ANY)
    out = pl.BlockSpec(memory_space=pltpu.VMEM)
    gg, gu, gd, gp, ig = pl.pallas_call(
        kernel,
        out_shape=(
            jax.ShapeDtypeStruct((448, 512), BF16),
            jax.ShapeDtypeStruct((448, 512), BF16),
            jax.ShapeDtypeStruct((448, 512), BF16),
            jax.ShapeDtypeStruct((512, 512), BF16),
            jax.ShapeDtypeStruct((128, 256), F32),
        ),
        in_specs=[anyspec] * 10,
        out_specs=(out,) * 5,
        scratch_shapes=[
            vmem((128, 4096), BF16),
            vmem((1, 4096), F32),
            vmem((448, 4096), BF16),
            vmem((448, 4096), BF16),
            vmem((448, 4096), BF16),
            vmem((512, 4096), BF16),
            vmem((1024, 1024), BF16),
            vmem((1024, 896), BF16),
            vmem((1024, 896), BF16),
            vmem((896, 1024), BF16),
            vmem((1024, 896), BF16),
            vmem((4, 2, 128, 1792), BF16),
            vmem((4, 128, 1792), BF16),
            vmem((6, 64, 1792), BF16),
            vmem((896, 1024), BF16),
            vmem((4, 4, 4, 128, 128), BF16),
            vmem((2, 6, 4, 128, 128), BF16),
            vmem((2, 2, 4, 128, 128), BF16),
            vmem((2, 6, 128, 128), BF16),
            vmem((3, 4, 4, 4, 32, 256), BF16),
            vmem((3, 2, 6, 4, 32, 256), BF16),
            vmem((3, 2, 2, 4, 32, 256), BF16),
            vmem((3, 2, 6, 32, 256), BF16),
            vmem((4, 4, 4, 32, 256), BF16),
            vmem((4, 4, 4, 32, 256), BF16),
            vmem((4, 4, 4, 32, 256), BF16),
            vmem((4, 4, 4, 32, 256), BF16),
            vmem((4, 4, 4, 32, 256), BF16),
            vmem((4, 4, 4, 32, 256), BF16),
            vmem((1024, 512), BF16),
            vmem((448, 1024), BF16),
            vmem((512, 1024), BF16),
            vmem((896, 1024), BF16),
            vmem((448, 128), F32),
            vmem((448, 128), F32),
            vmem((448, 128), F32),
            vmem((512, 128), F32),
            vmem((448, 128), F32),
            vmem((4, 128, 128), BF16),
            vmem((512, 128), BF16),
            vmem((128, 256), F32),
            vmem((128, 128), F32),
            vmem((4, 8, 128), F32),
            vmem((4, 8, 128), F32),
            vmem((128, 128), F32),
            pltpu.SemaphoreType.DMA((10,)),
            pltpu.SemaphoreType.DMA((SEMS,)),
            pltpu.SemaphoreType.DMA((SEMS,)),
        ],
        compiler_params=pltpu.CompilerParams(
            collective_id=0, has_side_effects=True, vmem_limit_bytes=67043328
        ),
    )(
        student_in,
        norm_gain.reshape(1, -1),
        gate_weight.T,
        up_weight.T,
        down_weight,
        projection.transpose(1, 2, 0).reshape(512, -1),
        teacher_in,
        teacher_gate,
        teacher_up,
        teacher_down,
    )
    return gg.T, gu.T, gd, gp.reshape(8, 64, 512).transpose(2, 0, 1), ig


def solution(mesh):
    split = Mesh(mesh.devices.reshape(2, 4, 2, 2, 4), ("zh", "y", "c", "zl", "x"))
    in_specs = (
        P(WID, None),
        P(),
        P(None, GH),
        P(None, GH),
        P(GH, None),
        P(None, None, GH),
        P(None, WID),
        P(WID, GH),
        P(WID, GH),
        P(GH, WID),
    )
    out_specs = (
        P(WID, GH),
        P(WID, GH),
        P(GH, WID),
        P(WID, None, GH),
        P(WID, GH),
    )
    return jax.shard_map(
        shards, mesh=split, in_specs=in_specs, out_specs=out_specs, check_vma=False
    )
```

```python
import jax
import jax.numpy as jnp
from jax import lax
from jax.experimental import pallas as pl
from jax.experimental.pallas import tpu as pltpu
from jax.sharding import Mesh
from jax.sharding import PartitionSpec as P

MESH = pl.DeviceIdType.MESH
F32 = jnp.float32
BF16 = jnp.bfloat16
WID = ("y", "c")
GH = ("zh", "zl", "x")
SEMS = 86

NN = (((1,), (0,)), ((), ()))
NT = (((1,), (1,)), ((), ()))
TN = (((0,), (0,)), ((), ()))


def mm(a, b, dims):
    return lax.dot_general(a, b, dims, preferred_element_type=F32)


def up(v):
    return v.astype(F32)


def mod4(v):
    return lax.rem(v, 4)


class Net:
    def __init__(self, send, recv):
        zh, y, c, zl, x = [lax.axis_index(a) for a in ("zh", "y", "c", "zl", "x")]
        self.z, self.x, self.y, self.c = zh * 2 + zl, x, y, c
        self.send, self.recv, self.copies, self.count = send, recv, [], 0

    def at(self, z=None, x=None, y=None, c=None):
        z = self.z if z is None else z
        return {
            "zh": lax.div(z, 2),
            "zl": lax.rem(z, 2),
            "x": self.x if x is None else x,
            "y": self.y if y is None else y,
            "c": self.c if c is None else c,
        }

    def along(self, axis, offset):
        return self.at(**{axis: mod4(getattr(self, axis) + offset)})

    def make(self, src, dst, peer, i):
        return pltpu.make_async_remote_copy(
            src_ref=src,
            dst_ref=dst,
            send_sem=self.send.at[i],
            recv_sem=self.recv.at[i],
            device_id=peer,
            device_id_type=MESH,
        )

    def slots(self, n):
        self.count += n
        return self.count - n

    def put(self, src, dst, peer):
        copy = self.make(src, dst, peer, self.slots(1))
        copy.start()
        self.copies.append(copy)
        return copy

    def group(self, size):
        whole = self.make(size, size, self.at(c=1 - self.c), self.slots(1))
        self.copies.append(whole)
        return Group(self, whole, self.count - 1)


class Group:
    def __init__(self, net, whole, i):
        self.net, self.whole, self.i = net, whole, i

    def put(self, src, dst, peer):
        self.net.make(src, dst, peer, self.i).start()

    def wait_recv(self):
        self.whole.wait_recv()


class RingSum:
    def __init__(self, net, axis, src, buf):
        self.net, self.axis, self.src, self.buf = net, axis, src, buf
        me = getattr(net, axis)
        self.me, self.r, self.o, self.l = me, mod4(me + 1), mod4(me + 2), mod4(me + 3)
        self.right, self.left = net.along(axis, 1), net.along(axis, 3)

    def far(self):
        self.m1 = self.net.put(self.src(self.o, 0), self.buf.at[0], self.right)
        self.n1 = self.net.put(self.src(self.o, 1), self.buf.at[1], self.left)

    def near_r(self):
        self.m2 = self.net.put(self.src(self.r, 1), self.buf.at[2], self.right)

    def near_l(self):
        self.n2 = self.net.put(self.src(self.l, 0), self.buf.at[3], self.left)

    def start(self):
        self.far()
        self.near_r()
        self.near_l()

    def relay(self):
        buf = self.buf
        self.m1.wait_recv()
        buf[0] = (up(buf[0]) + up(self.src(self.r, 0)[...])).astype(BF16)
        self.m3 = self.net.put(buf.at[0], buf.at[4], self.right)
        self.n1.wait_recv()
        buf[1] = (up(buf[1]) + up(self.src(self.l, 1)[...])).astype(BF16)
        self.n3 = self.net.put(buf.at[1], buf.at[5], self.left)

    def finish(self):
        buf = self.buf
        self.n2.wait_recv()
        self.m3.wait_recv()
        first = up(self.src(self.me, 0)[...]) + up(buf[3]) + up(buf[4])
        self.m2.wait_recv()
        self.n3.wait_recv()
        second = up(self.src(self.me, 1)[...]) + up(buf[2]) + up(buf[5])
        return first, second


class PlaneSum:
    def __init__(self, net, axes, src, buf1, mid, buf2):
        self.net, self.axes, self.src = net, axes, src
        self.buf1, self.mid, self.buf2 = buf1, mid, buf2

    def deal(self, axis, src, buf):
        me = getattr(self.net, axis)
        group = self.net.group(buf)
        for o in (2, 1, 3):
            group.put(src(mod4(me + o)), buf.at[o - 1], self.net.along(axis, o))
        return group

    def total(self, group, own, buf):
        group.wait_recv()
        return up(own[...]) + up(buf[0]) + up(buf[1]) + up(buf[2])

    def start(self):
        self.one = self.deal(self.axes[0], self.src, self.buf1)

    def turn(self):
        me = getattr(self.net, self.axes[0])
        self.mid[...] = self.total(self.one, self.src(me), self.buf1).astype(BF16)
        self.second()

    def second(self):
        self.two = self.deal(self.axes[1], lambda d: self.mid.at[d], self.buf2)

    def finish(self):
        me = getattr(self.net, self.axes[1])
        return self.total(self.two, self.mid.at[me], self.buf2)


class PlaneAll:
    def __init__(self, net, data, sizes):
        self.net, self.data, self.sizes = net, data, sizes

    def copies(self, piece, axis, size):
        group = self.net.group(size)
        for o in (2, 1, 3):
            group.put(piece, piece, self.net.along(axis, o))
        return group

    def start(self):
        z, x, size = self.net.z, self.net.x, self.sizes[0]
        self.a = self.copies(self.data.at[z, x, pl.ds(0, 2)], "z", size)
        self.b = self.copies(self.data.at[z, x, pl.ds(2, 2)], "x", size)

    def turn(self):
        z, x, size = self.net.z, self.net.x, self.sizes[1]
        self.a.wait_recv()
        self.a = self.copies(self.data.at[:, x, pl.ds(0, 2)], "x", size)
        self.b.wait_recv()
        self.b = self.copies(self.data.at[z, :, pl.ds(2, 2)], "z", size)

    def finish(self):
        self.a.wait_recv()
        self.b.wait_recv()


class TokenDirect:
    def __init__(self, net, data):
        self.net, self.data = net, data
        self.own = self.slot(0)

    def slot(self, o):
        at = pl.multiple_of((mod4(self.net.y + o) * 2 + self.net.c) * 128, 128)
        return self.data.at[:, pl.ds(at, 128)]

    def start(self):
        net, own = self.net, self.own
        self.mate = net.at(c=1 - net.c)
        self.far = [(4 - o, net.put(own, own, net.along("y", o))) for o in (2, 1, 3)]
        self.near = [net.put(own, own, self.mate)]

    def pass_on(self):
        for o, copy in self.far:
            copy.wait_recv()
            piece = self.slot(o)
            self.near.append(self.net.put(piece, piece, self.mate))

    def finish(self):
        for copy in self.near:
            copy.wait_recv()


class TokenAll:
    def __init__(self, net, data):
        self.net, self.data, self.rows = net, data, data.shape[0]
        self.own = self.slot(0)
        self.mate = net.at(c=1 - net.c)
        self.mates = {}

    def slot(self, o, h=None):
        at = pl.multiple_of((mod4(self.net.y + o) * 2 + self.net.c) * 128, 128)
        if h is None:
            return self.data.at[:, pl.ds(at, 128)]
        half = self.rows // 2
        return self.data.at[pl.ds(h * half, half), pl.ds(at, 128)]

    def send(self, o, h, to):
        piece = self.slot(o, h)
        return self.net.put(piece, piece, self.net.along("y", to))

    def share(self, o):
        piece = self.slot(o)
        self.mates[o] = self.net.put(piece, piece, self.mate)

    def start(self):
        self.share(0)
        self.r0, self.l1 = self.send(0, 0, 1), self.send(0, 1, 3)
        self.r1, self.l0 = self.send(0, 1, 1), self.send(0, 0, 3)

    def relay(self):
        self.r0.wait_recv()
        self.rr = self.send(3, 0, 1)
        self.l1.wait_recv()
        self.ll = self.send(1, 1, 3)

    def near(self):
        self.l0.wait_recv()
        self.share(1)
        self.r1.wait_recv()
        self.share(3)

    def finish(self):
        self.rr.wait_recv()
        self.ll.wait_recv()
        self.share(2)

    def wait(self, o):
        self.mates[o].wait_recv()


class Direct:
    def __init__(self, net, source, data):
        self.net, self.source, self.data = net, source, data

        self.group = net.group(data.at[pl.ds(0, 7)])

    def start(self, offsets):
        net = self.net
        to = self.data.at[net.y * 2 + net.c]
        if 0 in offsets:
            to[...] = self.source[net.y, pl.ds(2 * net.c, 2)]
        for o in offsets:
            for flip in (0, 1):
                if o or flip:
                    y, c = mod4(net.y + o), lax.rem(net.c + flip, 2)
                    piece = self.source.at[y, pl.ds(2 * c, 2)]
                    self.group.put(piece, to, net.at(y=y, c=c))

    def unpack(self, out):
        self.group.wait_recv()

        def body(w, _):
            rows = pl.ds(pl.multiple_of(w * 128, 128), 128)
            for half in (0, 1):
                out[rows, 256 * half : 256 * half + 256] = self.data[w, half].reshape(128, 256)
            return 0

        lax.fori_loop(0, 8, body, 0)


class Columns:
    def __init__(self, net, source, data, sizes):
        self.net, self.source, self.data = net, source, data
        self.plane = PlaneAll(net, data, sizes)

    def spread(self):
        net = self.net
        w, half = net.y * 2 + net.c, lax.div(net.x, 2)
        self.base, self.w = net.slots(8), w
        self.sent = []
        self.alone = jnp.logical_and(net.y == net.z, net.c == half)
        for o in range(4):
            for i in (0, 1):
                z, x = mod4(net.z + o), mod4(net.x + 2 * i)
                rows = pl.ds(pl.multiple_of(lax.div(x, 2) * 16, 16), 16)
                piece = self.source.at[net.z, net.x, z, rows]
                to = self.data.at[z, x, net.y, pl.ds(pl.multiple_of(net.c * 16, 16), 16)]
                copy = pltpu.make_async_remote_copy(
                    src_ref=piece,
                    dst_ref=to,
                    send_sem=net.send.at[self.base + 2 * o + i],
                    recv_sem=net.recv.at[self.base + w],
                    device_id=net.at(z=z, x=x, y=net.z, c=half),
                    device_id_type=MESH,
                )
                self.sent.append(copy)
                if o or i:
                    copy.start()
                    net.copies.append(copy)
                else:
                    here = (piece, to)
        first, (piece, to) = self.sent[0], here

        @pl.when(self.alone)
        def _():
            to[...] = piece[...]

        @pl.when(jnp.logical_not(self.alone))
        def _():
            first.start()

    def wait_first(self):
        @pl.when(jnp.logical_not(self.alone))
        def _():
            self.sent[0].wait_send()

    def start(self):
        net = self.net
        for w in range(8):
            slot = self.data.at[net.z, net.x, w // 2, pl.ds(16 * (w % 2), 16)]
            copy = net.make(slot, slot, net.at(c=1 - net.c), self.base + w)

            @pl.when(jnp.logical_not(jnp.logical_and(self.alone, self.w == w)))
            def _():
                copy.wait_recv()

        self.plane.start()

    def unpack(self, out):
        data = self.data

        def body(y, _):
            for c in (0, 1):
                for half in (0, 1):
                    parts = [
                        data[z, 2 * i + half, y, 16 * c : 16 * c + 16]
                        for z in range(4)
                        for i in (0, 1)
                    ]
                    at = pl.multiple_of(y * 256 + c * 128, 128)
                    out[pl.ds(at, 128), 256 * half : 256 * half + 256] = jnp.concatenate(
                        parts, axis=0
                    )
            return 0

        lax.fori_loop(0, 4, body, 0)


def share_of(ref, z, x):
    return ref[z, x].reshape(128, 256)


def wide_of(ref, z):
    return jnp.concatenate([share_of(ref, z, x) for x in range(4)], axis=1)


def kernel(
    student_in,
    norm_gain,
    gate_weight,
    up_weight,
    down_weight,
    projection,
    teacher_in,
    teacher_gate,
    teacher_up,
    teacher_down,
    grad_gate,
    grad_up,
    grad_down,
    grad_proj,
    input_grad,
    xin,
    gain,
    wg,
    wu,
    wd,
    pj,
    tin,
    tg,
    tu,
    td,
    tdt,
    parts,
    mate,
    ring,
    thid,
    feat,
    feat1,
    featm,
    feat2,
    sums,
    sums1,
    summ,
    sums2,
    normed,
    summed,
    bgrad,
    ncols,
    scols,
    bcols,
    flat,
    nflat,
    hids,
    errs,
    ggs,
    gate,
    upsum,
    sigma,
    acc,
    acc2,
    tshare,
    target,
    fgrad,
    stat,
    statx,
    statz,
    invs,
    ogg,
    ogu,
    ogd,
    ogp,
    oig,
    load,
    store,
    send,
    recv,
):
    net = Net(send, recv)
    z, x, y, c = net.z, net.x, net.y, net.c
    ys = [mod4(y + o) for o in range(4)]

    loads = {}
    for i, (name, src, dst) in enumerate(
        (
            ("tin", teacher_in, tin),
            ("tg", teacher_gate, tg),
            ("tu", teacher_up, tu),
            ("xin", student_in, xin),
            ("gain", norm_gain, gain),
            ("wg", gate_weight, wg),
            ("wu", up_weight, wu),
            ("wd", down_weight, wd),
            ("td", teacher_down, td),
            ("pj", projection, pj),
        )
    ):
        loads[name] = pltpu.make_async_copy(src, dst, load.at[i])
        loads[name].start()

    barrier = pltpu.get_barrier_semaphore()
    peers = [net.at(y=mod4(y + o), c=lax.rem(c + f, 2)) for o in range(4) for f in (0, 1) if o or f]
    peers += [net.along("x", o) for o in (1, 2, 3)] + [net.along("z", o) for o in (1, 2, 3)]
    for peer in peers:
        pl.semaphore_signal(barrier, inc=1, device_id=peer, device_id_type=MESH)
    near = 2 * c + lax.rem(x, 2)
    for o in range(4):
        for f in (0, 1):
            source = net.at(z=y, x=near, y=mod4(y + o), c=lax.rem(c + f, 2))
            if o or f:
                pl.semaphore_signal(barrier, inc=1, device_id=source, device_id_type=MESH)
            else:

                @pl.when(jnp.logical_or(z != y, x != near))
                def _():
                    pl.semaphore_signal(barrier, inc=1, device_id=source, device_id_type=MESH)

    tsum = RingSum(
        net, "y", lambda d, h: parts.at[d, c, pl.ds(64 * h, 64)], ring
    )
    for name in ("tin", "tg", "tu"):
        loads[name].wait()
    pair = {}

    def project(o):
        d = ys[o]
        rows = tin[pl.ds(pl.multiple_of(d * 256, 256), 256), :]
        parts[d, :, :, 0:896] = mm(rows, tg[...], NN).astype(BF16).reshape(2, 128, 896)
        parts[d, :, :, 896:1792] = mm(rows, tu[...], NN).astype(BF16).reshape(2, 128, 896)

    def swap(o):
        d = ys[o]
        pair[o] = net.put(parts.at[d, 1 - c], mate.at[d], net.at(c=1 - c))

    def join(o):
        d = ys[o]
        pair[o].wait_recv()
        parts[d, c] = (up(parts[d, c]) + up(mate[d])).astype(BF16)

    project(2)
    own = jnp.logical_and(y == z, c == lax.div(x, 2)).astype(jnp.int32)
    pl.semaphore_wait(barrier, len(peers) + 8 - own)
    swap(2)
    project(1)
    swap(1)
    join(2)
    tsum.far()
    project(3)
    swap(3)
    join(1)
    tsum.near_r()

    loads["xin"].wait()
    loads["gain"].wait()

    def squares(b, total):
        v = up(xin[:, pl.ds(pl.multiple_of(b * 256, 256), 256)])
        return total + v * v

    total = lax.fori_loop(0, 16, squares, jnp.zeros((128, 256), F32))
    inv = lax.rsqrt(jnp.sum(total, axis=1, keepdims=True) / 4096.0 + 1e-05)
    invs[...] = jnp.broadcast_to(inv, (128, 128))

    def norm(b, _):
        at = pl.ds(pl.multiple_of(b * 256, 256), 256)
        scale = jnp.concatenate([invs[...], invs[...]], axis=1)
        v = up(xin[:, at]) * scale * gain[:, at]
        normed[lax.div(b, 4), lax.rem(b, 4)] = v.astype(BF16).reshape(4, 32, 256)
        return 0

    lax.fori_loop(0, 16, norm, 0)

    for name in ("wg", "wu", "wd"):
        loads[name].wait()

    def students(first, second, source, out_first, out_second):
        def body(b, _):
            at = pl.ds(pl.multiple_of(b * 1024, 1024), 1024)
            wide = wide_of(source, b)
            out_first[...] += mm(first[:, at], wide, NT)
            if second is not None:
                out_second[...] += mm(second[:, at], wide, NT)
            return 0

        out_first[...] = jnp.zeros(out_first.shape, F32)
        if second is not None:
            out_second[...] = jnp.zeros(out_second.shape, F32)
        lax.fori_loop(0, 4, body, 0)

    def back(out, pairs):
        def body(b, _):
            at = pl.ds(pl.multiple_of(b * 1024, 1024), 1024)
            v = sum(mm(small, w[:, at], TN) for small, w in pairs).astype(BF16)
            for i in range(4):
                out[b, i] = v[:, 256 * i : 256 * i + 256].reshape(4, 32, 256)
            return 0

        lax.fori_loop(0, 4, body, 0)

    def plane_sums(n):
        data = sums.at[n]
        q = (pl.ds(0, 2), pl.ds(2, 2))
        return [
            PlaneSum(
                net,
                ("x", "z"),
                lambda d: data.at[:, d, q[0]],
                sums1.at[n, 0],
                summ.at[n, 0],
                sums2.at[n, 0],
            ),
            PlaneSum(
                net,
                ("z", "x"),
                lambda d: data.at[d, :, q[1]],
                sums1.at[n, 1],
                summ.at[n, 1],
                sums2.at[n, 1],
            ),
        ]

    students(wg, wu, normed, gate, upsum)
    join(3)
    tsum.near_l()
    sig = jax.nn.sigmoid(gate[...])
    sigma[...] = sig
    hid = (gate[...] * sig * upsum[...]).astype(BF16)
    hiddens = TokenDirect(net, hids)
    hiddens.own[...] = hid
    back(sums.at[0], ((hid, wd),))
    branch = plane_sums(0)
    for s in branch:
        s.start()
    tsum.relay()
    project(0)
    swap(0)
    loads["td"].wait()
    tdt[...] = td[...].T
    join(0)
    for s in branch:
        s.turn()

    first, second = tsum.finish()
    sums_all = jnp.concatenate([first, second], axis=0)
    g = sums_all[:, :896]
    teach = g * jax.nn.sigmoid(g) * sums_all[:, 896:]
    teachers = TokenAll(net, thid)
    teachers.own[...] = teach.T.astype(BF16)
    teachers.start()

    order = [ys[0], ys[1], ys[3], ys[2]]

    def group(k):
        d = order[k]
        if k % 2 == 0:
            axes, src = ("x", "z"), lambda e: feat.at[:, e, d]
        else:
            axes, src = ("z", "x"), lambda e: feat.at[e, :, d]
        return PlaneSum(net, axes, src, feat1.at[k], featm.at[k], feat2.at[k])

    teaching = [group(k) for k in range(4)]

    def feature(k, o):
        d = ys[o]
        teachers.wait(o)
        v = mm(tdt[...], thid[:, pl.ds(pl.multiple_of(d * 256, 256), 256)], NN).astype(BF16)
        for f in (0, 1):
            feat[:, :, d, 64 * f : 64 * f + 64] = v[:, 128 * f : 128 * f + 128].reshape(
                4, 4, 64, 128
            )
        teaching[k].start()

    rows_of = lambda j: pl.ds(64 * j, 64)
    share_at = pl.ds(pl.multiple_of((z * 4 + x) * 256, 256), 256)
    for j in (0, 1):
        v = branch[j].finish().reshape(64, 256)
        summed[z, x, 2 * j : 2 * j + 2] = (
            (up(xin[rows_of(j), share_at]) + v).astype(BF16).reshape(2, 32, 256)
        )
    sizes = (sums2.at[0, 0], sums1.at[0, 0])
    sum_all = PlaneAll(net, summed, sizes)
    sum_all.start()
    feature(0, 0)
    teachers.relay()
    sum_all.turn()
    teachers.near()
    feature(1, 1)
    feature(2, 3)
    teachers.finish()
    feature(3, 2)
    teaching[0].turn()
    ncol = Direct(net, normed, ncols)
    ncol.start((2, 0))
    sum_all.finish()
    loads["pj"].wait()
    students(pj, None, summed, acc, None)

    sent = net.group(target.at[pl.ds(0, 448)])

    def hand(k, v):
        d = order[k]
        tshare[d] = v.astype(BF16)
        to = target.at[pl.ds(pl.multiple_of((y * 2 + c) * 64, 64), 64)]
        for f in (0, 1):
            cc = lax.rem(c + f, 2)
            piece = tshare.at[d, pl.ds(pl.multiple_of(cc * 64, 64), 64)]
            if k == 0 and f == 0:
                to[...] = piece[...]
            else:
                sent.put(piece, to, net.at(y=d, c=cc))

    teaching[1].turn()
    hand(0, teaching[0].finish())
    teaching[2].turn()
    hand(1, teaching[1].finish())
    teaching[3].turn()
    hand(2, teaching[2].finish())
    hand(3, teaching[3].finish())
    sent.wait_recv()

    err = ((acc[...] - up(target[...])) * (1.0 / 32.0)).astype(BF16)
    errors = TokenDirect(net, errs)
    errors.own[...] = err
    errors.start()
    back(sums.at[1], ((err, pj),))
    grads = plane_sums(1)
    for s in grads:
        s.start()
    scol = Direct(net, summed, scols)
    scol.start((2, 0))
    for s in grads:
        s.turn()
    for j in (0, 1):
        v = grads[j].finish()
        fgrad[rows_of(j), :] = v.reshape(64, 256)
        bgrad[z, x, 2 * j : 2 * j + 2] = v.astype(BF16)
    grad_all = PlaneAll(net, bgrad, sizes)
    grad_all.start()
    bcol = Columns(net, bgrad, bcols, sizes)
    bcol.spread()
    errors.pass_on()
    scol.start((1, 3))
    hiddens.start()
    grad_all.turn()
    errors.finish()
    bcol.start()
    grad_all.finish()

    students(wd, None, bgrad, acc2, None)
    hg = acc2[...]
    g, s = gate[...], sigma[...]
    gg = (hg * upsum[...] * s * (1.0 + g * (1.0 - s))).astype(BF16)
    ug = (hg * g * s).astype(BF16)
    moment = jnp.sum(up(gg) * g + up(ug) * upsum[...], axis=0, keepdims=True)
    gates = TokenDirect(net, ggs)
    own_at = pl.ds(pl.multiple_of((y * 2 + c) * 128, 128), 128)
    ggs[0:448, own_at] = gg
    ggs[448:896, own_at] = ug
    gates.start()
    ncol.start((1, 3))

    def tell(ref, me, axis):
        group = net.group(ref.at[pl.ds(0, 3)])
        for o in (2, 1, 3):
            group.put(ref.at[me], ref.at[me], net.along(axis, o))
        return group

    statx[x] = jnp.broadcast_to(moment, (8, 128))
    stats = tell(statx, x, "x")
    bcol.plane.turn()
    back(sums.at[2], ((gg, wg), (ug, wu)))
    inner = plane_sums(2)
    for s in inner:
        s.start()
    stats.wait_recv()
    statz[z] = statx[0] + statx[1] + statx[2] + statx[3]
    stats = tell(statz, z, "z")
    hiddens.pass_on()
    scol.unpack(flat)

    outs = []

    def write(i, src, dst):
        outs.append(pltpu.make_async_copy(src, dst, store.at[i]))
        outs[-1].start()

    ogp[...] = mm(errs[...], flat[...], NN).astype(BF16)
    write(0, ogp, grad_proj)
    for s in inner:
        s.turn()
    stats.wait_recv()
    whole = (statz[0] + statz[1] + statz[2] + statz[3]) / 4096.0
    stat[...] = jnp.broadcast_to(whole[0:1], (128, 128)).T
    gates.pass_on()
    for j in (0, 1):
        v = inner[j].finish().reshape(64, 256)
        r = rows_of(j)
        scale = jnp.concatenate([invs[r, :], invs[r, :]], axis=1)
        mean = jnp.concatenate([stat[r, :], stat[r, :]], axis=1)
        scaled = v * gain[:, share_at]
        oig[r, :] = fgrad[r, :] + scale * (scaled - up(xin[r, share_at]) * scale * mean)
    write(1, oig, input_grad)
    gates.finish()
    ncol.unpack(nflat)
    ogg[...] = mm(ggs[0:448], nflat[...], NN).astype(BF16)
    write(2, ogg, grad_gate)
    ogu[...] = mm(ggs[448:896], nflat[...], NN).astype(BF16)
    write(3, ogu, grad_up)
    bcol.plane.finish()
    bcol.unpack(flat)
    hiddens.finish()
    ogd[...] = mm(hids[...], flat[...], NN).astype(BF16)
    write(4, ogd, grad_down)
    bcol.wait_first()
    for copy in net.copies:
        copy.wait_send()
    for copy in outs:
        copy.wait()


def move(*refs):
    srcs, dsts, held = refs[0:5], refs[5:10], refs[10:15]
    came, went = refs[15], refs[16]
    ins = [pltpu.make_async_copy(s, h, came.at[i]) for i, (s, h) in enumerate(zip(srcs, held))]
    outs = [pltpu.make_async_copy(h, d, went.at[i]) for i, (h, d) in enumerate(zip(held, dsts))]
    for copy in ins:
        copy.start()
    for i, copy in zip(ins, outs):
        i.wait()
        copy.start()
    for copy in outs:
        copy.wait()


def shards(
    student_in,
    norm_gain,
    gate_weight,
    up_weight,
    down_weight,
    projection,
    teacher_in,
    teacher_gate,
    teacher_up,
    teacher_down,
):
    vmem = pltpu.VMEM
    anyspec = pl.BlockSpec(memory_space=pl.ANY)
    shapes = (
        jax.ShapeDtypeStruct((448, 512), BF16),
        jax.ShapeDtypeStruct((448, 512), BF16),
        jax.ShapeDtypeStruct((448, 512), BF16),
        jax.ShapeDtypeStruct((512, 512), BF16),
        jax.ShapeDtypeStruct((128, 256), F32),
    )
    made = pl.pallas_call(
        kernel,
        out_shape=shapes,
        in_specs=[anyspec] * 10,
        out_specs=(anyspec,) * 5,
        scratch_shapes=[
            vmem((128, 4096), BF16),
            vmem((1, 4096), F32),
            vmem((448, 4096), BF16),
            vmem((448, 4096), BF16),
            vmem((448, 4096), BF16),
            vmem((512, 4096), BF16),
            vmem((1024, 1024), BF16),
            vmem((1024, 896), BF16),
            vmem((1024, 896), BF16),
            vmem((896, 1024), BF16),
            vmem((1024, 896), BF16),
            vmem((4, 2, 128, 1792), BF16),
            vmem((4, 128, 1792), BF16),
            vmem((6, 64, 1792), BF16),
            vmem((896, 1024), BF16),
            vmem((4, 4, 4, 128, 128), BF16),
            vmem((4, 3, 4, 128, 128), BF16),
            vmem((4, 4, 128, 128), BF16),
            vmem((4, 3, 128, 128), BF16),
            vmem((3, 4, 4, 4, 32, 256), BF16),
            vmem((3, 2, 3, 4, 2, 32, 256), BF16),
            vmem((3, 2, 4, 2, 32, 256), BF16),
            vmem((3, 2, 3, 2, 32, 256), BF16),
            vmem((4, 4, 4, 32, 256), BF16),
            vmem((4, 4, 4, 32, 256), BF16),
            vmem((4, 4, 4, 32, 256), BF16),
            vmem((8, 2, 4, 32, 256), BF16),
            vmem((8, 2, 4, 32, 256), BF16),
            vmem((4, 4, 4, 32, 256), BF16),
            vmem((1024, 512), BF16),
            vmem((1024, 512), BF16),
            vmem((448, 1024), BF16),
            vmem((512, 1024), BF16),
            vmem((896, 1024), BF16),
            vmem((448, 128), F32),
            vmem((448, 128), F32),
            vmem((448, 128), F32),
            vmem((512, 128), F32),
            vmem((448, 128), F32),
            vmem((4, 128, 128), BF16),
            vmem((512, 128), BF16),
            vmem((128, 256), F32),
            vmem((128, 128), F32),
            vmem((4, 8, 128), F32),
            vmem((4, 8, 128), F32),
            vmem((128, 128), F32),
            vmem((448, 512), BF16),
            vmem((448, 512), BF16),
            vmem((448, 512), BF16),
            vmem((512, 512), BF16),
            vmem((128, 256), F32),
            pltpu.SemaphoreType.DMA((10,)),
            pltpu.SemaphoreType.DMA((5,)),
            pltpu.SemaphoreType.DMA((SEMS,)),
            pltpu.SemaphoreType.DMA((SEMS,)),
        ],
        compiler_params=pltpu.CompilerParams(
            collective_id=0, has_side_effects=True, vmem_limit_bytes=67043328
        ),
    )(
        student_in,
        norm_gain.reshape(1, -1),
        gate_weight.T,
        up_weight.T,
        down_weight,
        projection.transpose(1, 2, 0).reshape(512, -1),
        teacher_in,
        teacher_gate,
        teacher_up,
        teacher_down,
    )
    gg, gu, gd, gp, ig = pl.pallas_call(
        move,
        out_shape=shapes,
        in_specs=[anyspec] * 5,
        out_specs=(anyspec,) * 5,
        scratch_shapes=[vmem(s.shape, s.dtype) for s in shapes]
        + [pltpu.SemaphoreType.DMA((5,)), pltpu.SemaphoreType.DMA((5,))],
    )(*made)
    return gg.T, gu.T, gd, gp.reshape(8, 64, 512).transpose(2, 0, 1), ig


def solution(mesh):
    split = Mesh(mesh.devices.reshape(2, 4, 2, 2, 4), ("zh", "y", "c", "zl", "x"))
    in_specs = (
        P(WID, None),
        P(),
        P(None, GH),
        P(None, GH),
        P(GH, None),
        P(None, None, GH),
        P(None, WID),
        P(WID, GH),
        P(WID, GH),
        P(GH, WID),
    )
    out_specs = (
        P(WID, GH),
        P(WID, GH),
        P(GH, WID),
        P(WID, None, GH),
        P(WID, GH),
    )
    return jax.shard_map(
        shards, mesh=split, in_specs=in_specs, out_specs=out_specs, check_vma=False
    )
```

```python
import jax
import jax.numpy as jnp
from jax import lax
from jax.experimental import pallas as pl
from jax.experimental.pallas import tpu as pltpu
from jax.sharding import Mesh
from jax.sharding import PartitionSpec as P

MESH = pl.DeviceIdType.MESH
F32 = jnp.float32
BF16 = jnp.bfloat16
WID = ("y", "c")
GH = ("zh", "zl", "x")
SEMS = 95
ORDER = (0, 2, 1, 3)

NN = (((1,), (0,)), ((), ()))
NT = (((1,), (1,)), ((), ()))
TN = (((0,), (0,)), ((), ()))


def mm(a, b, dims):
    return lax.dot_general(a, b, dims, preferred_element_type=F32)


def up(v):
    return v.astype(F32)


def mod4(v):
    return lax.rem(v, 4)


class Net:
    def __init__(self, send, recv):
        zh, y, c, zl, x = [lax.axis_index(a) for a in ("zh", "y", "c", "zl", "x")]
        self.z, self.x, self.y, self.c = zh * 2 + zl, x, y, c
        self.send, self.recv, self.copies, self.count = send, recv, [], 0

    def at(self, z=None, x=None, y=None, c=None):
        z = self.z if z is None else z
        return {
            "zh": lax.div(z, 2),
            "zl": lax.rem(z, 2),
            "x": self.x if x is None else x,
            "y": self.y if y is None else y,
            "c": self.c if c is None else c,
        }

    def along(self, axis, offset):
        return self.at(**{axis: mod4(getattr(self, axis) + offset)})

    def make(self, src, dst, peer, i):
        return pltpu.make_async_remote_copy(
            src_ref=src,
            dst_ref=dst,
            send_sem=self.send.at[i],
            recv_sem=self.recv.at[i],
            device_id=peer,
            device_id_type=MESH,
        )

    def slots(self, n):
        self.count += n
        return self.count - n

    def put(self, src, dst, peer):
        copy = self.make(src, dst, peer, self.slots(1))
        copy.start()
        self.copies.append(copy)
        return copy

    def group(self, size):
        whole = self.make(size, size, self.at(c=1 - self.c), self.slots(1))
        self.copies.append(whole)
        return Group(self, whole, self.count - 1)


class Group:
    def __init__(self, net, whole, i):
        self.net, self.whole, self.i = net, whole, i

    def put(self, src, dst, peer):
        self.net.make(src, dst, peer, self.i).start()

    def wait_recv(self):
        self.whole.wait_recv()


class RingSum:
    def __init__(self, net, axis, src, buf):
        self.net, self.axis, self.src, self.buf = net, axis, src, buf
        me = getattr(net, axis)
        self.me, self.r, self.o, self.l = me, mod4(me + 1), mod4(me + 2), mod4(me + 3)
        self.right, self.left = net.along(axis, 1), net.along(axis, 3)

    def far(self):
        self.m1 = self.net.put(self.src(self.o, 0), self.buf.at[0], self.right)
        self.n1 = self.net.put(self.src(self.o, 1), self.buf.at[1], self.left)

    def near_r(self):
        self.m2 = self.net.put(self.src(self.r, 1), self.buf.at[2], self.right)

    def near_l(self):
        self.n2 = self.net.put(self.src(self.l, 0), self.buf.at[3], self.left)

    def start(self):
        self.far()
        self.near_r()
        self.near_l()

    def relay(self):
        buf = self.buf
        self.m1.wait_recv()
        buf[0] = (up(buf[0]) + up(self.src(self.r, 0)[...])).astype(BF16)
        self.m3 = self.net.put(buf.at[0], buf.at[4], self.right)
        self.n1.wait_recv()
        buf[1] = (up(buf[1]) + up(self.src(self.l, 1)[...])).astype(BF16)
        self.n3 = self.net.put(buf.at[1], buf.at[5], self.left)

    def finish(self):
        buf = self.buf
        self.n2.wait_recv()
        self.m3.wait_recv()
        first = up(self.src(self.me, 0)[...]) + up(buf[3]) + up(buf[4])
        self.m2.wait_recv()
        self.n3.wait_recv()
        second = up(self.src(self.me, 1)[...]) + up(buf[2]) + up(buf[5])
        return first, second


class PlaneSum:
    def __init__(self, net, axes, src, buf1, mid, buf2):
        self.net, self.axes, self.src = net, axes, src
        self.buf1, self.mid, self.buf2 = buf1, mid, buf2

    def deal(self, axis, src, buf):
        me = getattr(self.net, axis)
        group = self.net.group(buf)
        for o in (2, 1, 3):
            group.put(src(mod4(me + o)), buf.at[o - 1], self.net.along(axis, o))
        return group

    def total(self, group, own, buf):
        group.wait_recv()
        return up(own[...]) + up(buf[0]) + up(buf[1]) + up(buf[2])

    def start(self):
        self.one = self.deal(self.axes[0], self.src, self.buf1)

    def turn(self):
        me = getattr(self.net, self.axes[0])
        self.mid[...] = self.total(self.one, self.src(me), self.buf1).astype(BF16)
        self.second()

    def second(self):
        self.two = self.deal(self.axes[1], lambda d: self.mid.at[d], self.buf2)

    def finish(self):
        me = getattr(self.net, self.axes[1])
        return self.total(self.two, self.mid.at[me], self.buf2)


class PlaneAll:
    def __init__(self, net, data, sizes):
        self.net, self.data, self.sizes, self.groups = net, data, sizes, {}

    def copies(self, q, piece, axis, size):
        group = self.groups[q] = self.net.group(size)
        for o in (2, 1, 3):
            group.put(piece, piece, self.net.along(axis, o))

    def start(self, *blocks):
        for q in blocks:
            piece = self.data.at[self.net.z, self.net.x, q]
            self.copies(q, piece, "z" if q < 2 else "x", self.sizes[0])

    def turn(self, *blocks):
        for q in blocks:
            self.groups[q].wait_recv()
            if q < 2:
                self.copies(q, self.data.at[:, self.net.x, q], "x", self.sizes[1])
            else:
                self.copies(q, self.data.at[self.net.z, :, q], "z", self.sizes[1])

    def finish(self):
        for q in ORDER:
            self.groups[q].wait_recv()


class TokenDirect:
    def __init__(self, net, data):
        self.net, self.data = net, data
        self.own = self.slot(0)

    def slot(self, o):
        at = pl.multiple_of((mod4(self.net.y + o) * 2 + self.net.c) * 128, 128)
        return self.data.at[:, pl.ds(at, 128)]

    def start(self):
        net, own = self.net, self.own
        self.mate = net.at(c=1 - net.c)
        self.far = net.group(self.data.at[:, pl.ds(0, 384)])
        self.near = net.group(self.data.at[:, pl.ds(0, 512)])
        for o in (2, 1, 3):
            self.far.put(own, own, net.along("y", o))
        self.near.put(own, own, self.mate)

    def pass_on(self):
        self.far.wait_recv()
        for o in (2, 1, 3):
            piece = self.slot(o)
            self.near.put(piece, piece, self.mate)

    def finish(self):
        self.near.wait_recv()


class TokenAll:
    def __init__(self, net, data):
        self.net, self.data, self.rows = net, data, data.shape[0]
        self.own = self.slot(0)
        self.mate = net.at(c=1 - net.c)
        self.mates = {}

    def slot(self, o, h=None):
        at = pl.multiple_of((mod4(self.net.y + o) * 2 + self.net.c) * 128, 128)
        if h is None:
            return self.data.at[:, pl.ds(at, 128)]
        half = self.rows // 2
        return self.data.at[pl.ds(h * half, half), pl.ds(at, 128)]

    def send(self, o, h, to):
        piece = self.slot(o, h)
        return self.net.put(piece, piece, self.net.along("y", to))

    def share(self, o):
        piece = self.slot(o)
        self.mates[o] = self.net.put(piece, piece, self.mate)

    def start(self):
        self.share(0)
        self.r0, self.l1 = self.send(0, 0, 1), self.send(0, 1, 3)
        self.r1, self.l0 = self.send(0, 1, 1), self.send(0, 0, 3)

    def relay(self):
        self.r0.wait_recv()
        self.rr = self.send(3, 0, 1)
        self.l1.wait_recv()
        self.ll = self.send(1, 1, 3)

    def near(self):
        self.l0.wait_recv()
        self.share(1)
        self.r1.wait_recv()
        self.share(3)

    def finish(self):
        self.rr.wait_recv()
        self.ll.wait_recv()
        self.share(2)

    def wait(self, o):
        self.mates[o].wait_recv()


class Direct:
    def __init__(self, net, source, data):
        self.net, self.source, self.data = net, source, data

        self.group = net.group(data.at[pl.ds(0, 7)])

    def start(self, offsets):
        net = self.net
        to = self.data.at[net.y * 2 + net.c]
        if 0 in offsets:
            to[...] = self.source[net.y, pl.ds(2 * net.c, 2)]
        for o in offsets:
            for flip in (0, 1):
                if o or flip:
                    y, c = mod4(net.y + o), lax.rem(net.c + flip, 2)
                    piece = self.source.at[y, pl.ds(2 * c, 2)]
                    self.group.put(piece, to, net.at(y=y, c=c))

    def unpack(self, out):
        self.group.wait_recv()

        def body(w, _):
            rows = pl.ds(pl.multiple_of(w * 128, 128), 128)
            for half in (0, 1):
                out[rows, 256 * half : 256 * half + 256] = self.data[w, half].reshape(128, 256)
            return 0

        lax.fori_loop(0, 8, body, 0)


class Columns:
    def __init__(self, net, source, data, sizes):
        self.net, self.source, self.data = net, source, data
        self.plane = PlaneAll(net, data, sizes)

    def spread(self):
        net = self.net
        w, half = net.y * 2 + net.c, lax.div(net.x, 2)
        self.base, self.w = net.slots(8), w
        self.sent = []
        self.alone = jnp.logical_and(net.y == net.z, net.c == half)
        for o in range(4):
            for i in (0, 1):
                z, x = mod4(net.z + o), mod4(net.x + 2 * i)
                rows = pl.ds(pl.multiple_of(lax.div(x, 2) * 16, 16), 16)
                piece = self.source.at[net.z, net.x, z, rows]
                to = self.data.at[z, x, net.y, pl.ds(pl.multiple_of(net.c * 16, 16), 16)]
                copy = pltpu.make_async_remote_copy(
                    src_ref=piece,
                    dst_ref=to,
                    send_sem=net.send.at[self.base + 2 * o + i],
                    recv_sem=net.recv.at[self.base + w],
                    device_id=net.at(z=z, x=x, y=net.z, c=half),
                    device_id_type=MESH,
                )
                self.sent.append(copy)
                if o or i:
                    copy.start()
                    net.copies.append(copy)
                else:
                    here = (piece, to)
        first, (piece, to) = self.sent[0], here

        @pl.when(self.alone)
        def _():
            to[...] = piece[...]

        @pl.when(jnp.logical_not(self.alone))
        def _():
            first.start()

    def wait_first(self):
        @pl.when(jnp.logical_not(self.alone))
        def _():
            self.sent[0].wait_send()

    def start(self):
        net = self.net
        for w in range(8):
            slot = self.data.at[net.z, net.x, w // 2, pl.ds(16 * (w % 2), 16)]
            copy = net.make(slot, slot, net.at(c=1 - net.c), self.base + w)

            @pl.when(jnp.logical_not(jnp.logical_and(self.alone, self.w == w)))
            def _():
                copy.wait_recv()

        self.plane.start(*ORDER)

    def unpack(self, out):
        data = self.data

        def body(y, _):
            for c in (0, 1):
                for half in (0, 1):
                    parts = [
                        data[z, 2 * i + half, y, 16 * c : 16 * c + 16]
                        for z in range(4)
                        for i in (0, 1)
                    ]
                    at = pl.multiple_of(y * 256 + c * 128, 128)
                    out[pl.ds(at, 128), 256 * half : 256 * half + 256] = jnp.concatenate(
                        parts, axis=0
                    )
            return 0

        lax.fori_loop(0, 4, body, 0)


def share_of(ref, z, x):
    return ref[z, x].reshape(128, 256)


def wide_of(ref, z):
    return jnp.concatenate([share_of(ref, z, x) for x in range(4)], axis=1)


def kernel(
    student_in,
    norm_gain,
    gate_weight,
    up_weight,
    down_weight,
    projection,
    teacher_in,
    teacher_gate,
    teacher_up,
    teacher_down,
    grad_gate,
    grad_up,
    grad_down,
    grad_proj,
    input_grad,
    xin,
    gain,
    wg,
    wu,
    wd,
    pj,
    tin,
    tg,
    tu,
    td,
    tdt,
    parts,
    mate,
    ring,
    thid,
    feat,
    feat1,
    featm,
    feat2,
    sums,
    sums1,
    summ,
    sums2,
    normed,
    summed,
    bgrad,
    ncols,
    scols,
    bcols,
    flat,
    nflat,
    hids,
    errs,
    ggs,
    gate,
    upsum,
    sigma,
    acc,
    acc2,
    tshare,
    target,
    fgrad,
    stat,
    statx,
    statz,
    invs,
    ogg,
    ogu,
    ogd,
    ogp,
    oig,
    load,
    store,
    send,
    recv,
):
    net = Net(send, recv)
    z, x, y, c = net.z, net.x, net.y, net.c
    ys = [mod4(y + o) for o in range(4)]

    rows_in = [pl.ds(pl.multiple_of(d * 256, 256), 256) for d in ys]
    loads = {}
    for i, (name, src, dst) in enumerate(
        (
            (2, teacher_in.at[rows_in[2]], tin.at[rows_in[2]]),
            ("tg", teacher_gate, tg),
            ("tu", teacher_up, tu),
            (1, teacher_in.at[rows_in[1]], tin.at[rows_in[1]]),
            (3, teacher_in.at[rows_in[3]], tin.at[rows_in[3]]),
            (0, teacher_in.at[rows_in[0]], tin.at[rows_in[0]]),
            ("xin", student_in, xin),
            ("gain", norm_gain, gain),
            ("wg", gate_weight, wg),
            ("wu", up_weight, wu),
            ("wd", down_weight, wd),
            ("td", teacher_down, td),
            ("pj", projection, pj),
        )
    ):
        loads[name] = pltpu.make_async_copy(src, dst, load.at[i])
        loads[name].start()

    barrier = pltpu.get_barrier_semaphore()
    peers = [net.at(y=mod4(y + o), c=lax.rem(c + f, 2)) for o in range(4) for f in (0, 1) if o or f]
    peers += [net.along("x", o) for o in (1, 2, 3)] + [net.along("z", o) for o in (1, 2, 3)]
    for peer in peers:
        pl.semaphore_signal(barrier, inc=1, device_id=peer, device_id_type=MESH)
    near = 2 * c + lax.rem(x, 2)
    for o in range(4):
        for f in (0, 1):
            source = net.at(z=y, x=near, y=mod4(y + o), c=lax.rem(c + f, 2))
            if o or f:
                pl.semaphore_signal(barrier, inc=1, device_id=source, device_id_type=MESH)
            else:

                @pl.when(jnp.logical_or(z != y, x != near))
                def _():
                    pl.semaphore_signal(barrier, inc=1, device_id=source, device_id_type=MESH)

    tsum = RingSum(
        net, "y", lambda d, h: parts.at[d, c, pl.ds(64 * h, 64)], ring
    )
    pair = {}

    def project(o):
        d = ys[o]
        loads[o].wait()
        rows = tin[rows_in[o], :]
        if o == 2:
            loads["tg"].wait()
        parts[d, :, :, 0:896] = mm(rows, tg[...], NN).astype(BF16).reshape(2, 128, 896)
        if o == 2:
            loads["tu"].wait()
        parts[d, :, :, 896:1792] = mm(rows, tu[...], NN).astype(BF16).reshape(2, 128, 896)

    def swap(o):
        d = ys[o]
        pair[o] = net.put(parts.at[d, 1 - c], mate.at[d], net.at(c=1 - c))

    def join(o):
        d = ys[o]
        pair[o].wait_recv()
        parts[d, c] = (up(parts[d, c]) + up(mate[d])).astype(BF16)

    project(2)
    own = jnp.logical_and(y == z, c == lax.div(x, 2)).astype(jnp.int32)
    pl.semaphore_wait(barrier, len(peers) + 8 - own)
    swap(2)
    project(1)
    swap(1)
    join(2)
    tsum.far()
    project(3)
    swap(3)
    join(1)
    tsum.near_r()

    loads["xin"].wait()
    loads["gain"].wait()

    def squares(b, total):
        v = up(xin[:, pl.ds(pl.multiple_of(b * 256, 256), 256)])
        return total + v * v

    total = lax.fori_loop(0, 16, squares, jnp.zeros((128, 256), F32))
    inv = lax.rsqrt(jnp.sum(total, axis=1, keepdims=True) / 4096.0 + 1e-05)
    invs[...] = jnp.broadcast_to(inv, (128, 128))

    def norm(b, _):
        at = pl.ds(pl.multiple_of(b * 256, 256), 256)
        scale = jnp.concatenate([invs[...], invs[...]], axis=1)
        v = up(xin[:, at]) * scale * gain[:, at]
        normed[lax.div(b, 4), lax.rem(b, 4)] = v.astype(BF16).reshape(4, 32, 256)
        return 0

    lax.fori_loop(0, 16, norm, 0)

    for name in ("wg", "wu", "wd"):
        loads[name].wait()

    def students(first, second, source, out_first, out_second):
        def body(b, _):
            at = pl.ds(pl.multiple_of(b * 1024, 1024), 1024)
            wide = wide_of(source, b)
            out_first[...] += mm(first[:, at], wide, NT)
            if second is not None:
                out_second[...] += mm(second[:, at], wide, NT)
            return 0

        out_first[...] = jnp.zeros(out_first.shape, F32)
        if second is not None:
            out_second[...] = jnp.zeros(out_second.shape, F32)
        lax.fori_loop(0, 4, body, 0)

    def back(out, pairs):
        def body(b, _):
            at = pl.ds(pl.multiple_of(b * 1024, 1024), 1024)
            v = sum(mm(small, w[:, at], TN) for small, w in pairs).astype(BF16)
            for i in range(4):
                out[b, i] = v[:, 256 * i : 256 * i + 256].reshape(4, 32, 256)
            return 0

        lax.fori_loop(0, 4, body, 0)

    def plane_sums(n):
        data = sums.at[n]

        def block(q):
            if q < 2:
                axes, src = ("x", "z"), lambda d: data.at[:, d, q]
            else:
                axes, src = ("z", "x"), lambda d: data.at[d, :, q]
            return PlaneSum(net, axes, src, sums1.at[n, q], summ.at[n, q], sums2.at[n, q])

        return [block(q) for q in range(4)]

    students(wg, wu, normed, gate, upsum)
    join(3)
    tsum.near_l()
    sig = jax.nn.sigmoid(gate[...])
    sigma[...] = sig
    hid = (gate[...] * sig * upsum[...]).astype(BF16)
    hiddens = TokenDirect(net, hids)
    hiddens.own[...] = hid
    back(sums.at[0], ((hid, wd),))
    branch = plane_sums(0)
    for q in ORDER:
        branch[q].start()
    tsum.relay()
    project(0)
    swap(0)
    loads["td"].wait()
    tdt[...] = td[...].T
    join(0)
    for q in ORDER:
        branch[q].turn()

    first, second = tsum.finish()
    sums_all = jnp.concatenate([first, second], axis=0)
    g = sums_all[:, :896]
    teach = g * jax.nn.sigmoid(g) * sums_all[:, 896:]
    teachers = TokenAll(net, thid)
    teachers.own[...] = teach.T.astype(BF16)
    teachers.start()

    order = [ys[0], ys[1], ys[3], ys[2]]

    def group(k):
        d = order[k]
        if k % 2 == 0:
            axes, src = ("x", "z"), lambda e: feat.at[:, e, d]
        else:
            axes, src = ("z", "x"), lambda e: feat.at[e, :, d]
        return PlaneSum(net, axes, src, feat1.at[k], featm.at[k], feat2.at[k])

    teaching = [group(k) for k in range(4)]

    def feature(k, o):
        d = ys[o]
        teachers.wait(o)
        v = mm(tdt[...], thid[:, pl.ds(pl.multiple_of(d * 256, 256), 256)], NN).astype(BF16)
        for f in (0, 1):
            feat[:, :, d, 64 * f : 64 * f + 64] = v[:, 128 * f : 128 * f + 128].reshape(
                4, 4, 64, 128
            )
        teaching[k].start()

    rows_of = lambda q: pl.ds(32 * q, 32)
    share_at = pl.ds(pl.multiple_of((z * 4 + x) * 256, 256), 256)
    sizes = (sums2.at[0, 0], sums1.at[0, 0])
    sum_all = PlaneAll(net, summed, sizes)
    for q in ORDER:
        v = branch[q].finish()
        summed[z, x, q] = (up(xin[rows_of(q), share_at]) + v).astype(BF16)
        sum_all.start(q)
    feature(0, 0)
    teachers.relay()
    sum_all.turn(*ORDER)
    teachers.near()
    feature(1, 1)
    feature(2, 3)
    teaching[0].turn()
    teachers.finish()
    feature(3, 2)
    ncol = Direct(net, normed, ncols)
    ncol.start((2, 1, 3, 0))
    sum_all.finish()
    loads["pj"].wait()
    students(pj, None, summed, acc, None)

    sent = net.group(target.at[pl.ds(0, 448)])

    def hand(k, v):
        d = order[k]
        tshare[d] = v.astype(BF16)
        to = target.at[pl.ds(pl.multiple_of((y * 2 + c) * 64, 64), 64)]
        for f in (0, 1):
            cc = lax.rem(c + f, 2)
            piece = tshare.at[d, pl.ds(pl.multiple_of(cc * 64, 64), 64)]
            if k == 0 and f == 0:
                to[...] = piece[...]
            else:
                sent.put(piece, to, net.at(y=d, c=cc))

    teaching[1].turn()
    teaching[2].turn()
    teaching[3].turn()
    for k in range(4):
        hand(k, teaching[k].finish())
    sent.wait_recv()

    err = ((acc[...] - up(target[...])) * (1.0 / 32.0)).astype(BF16)
    errors = TokenDirect(net, errs)
    errors.own[...] = err
    errors.start()
    back(sums.at[1], ((err, pj),))
    grads = plane_sums(1)
    for q in ORDER:
        grads[q].start()
    scol = Direct(net, summed, scols)
    scol.start((2, 0))
    for q in ORDER:
        grads[q].turn()
    grad_all = PlaneAll(net, bgrad, sizes)
    for q in ORDER:
        v = grads[q].finish()
        bgrad[z, x, q] = v.astype(BF16)
        grad_all.start(q)
        fgrad[rows_of(q), :] = v
    bcol = Columns(net, bgrad, bcols, sizes)
    bcol.spread()
    grad_all.turn(0, 2)
    errors.pass_on()
    scol.start((1, 3))
    hiddens.start()
    grad_all.turn(1, 3)
    errors.finish()
    bcol.start()
    grad_all.finish()

    students(wd, None, bgrad, acc2, None)
    hg = acc2[...]
    g, s = gate[...], sigma[...]
    gg = (hg * upsum[...] * s * (1.0 + g * (1.0 - s))).astype(BF16)
    ug = (hg * g * s).astype(BF16)
    moment = jnp.sum(up(gg) * g + up(ug) * upsum[...], axis=0, keepdims=True)
    gates = TokenDirect(net, ggs)
    own_at = pl.ds(pl.multiple_of((y * 2 + c) * 128, 128), 128)
    ggs[0:448, own_at] = gg
    ggs[448:896, own_at] = ug
    gates.start()

    def tell(ref, me, axis):
        group = net.group(ref.at[pl.ds(0, 3)])
        for o in (2, 1, 3):
            group.put(ref.at[me], ref.at[me], net.along(axis, o))
        return group

    statx[x] = jnp.broadcast_to(moment, (8, 128))
    stats = tell(statx, x, "x")
    bcol.plane.turn(0, 2)
    back(sums.at[2], ((gg, wg), (ug, wu)))
    inner = plane_sums(2)
    for q in ORDER:
        inner[q].start()
    bcol.plane.turn(1, 3)
    stats.wait_recv()
    statz[z] = statx[0] + statx[1] + statx[2] + statx[3]
    stats = tell(statz, z, "z")
    hiddens.pass_on()
    scol.unpack(flat)

    outs = []

    def write(i, src, dst):
        outs.append(pltpu.make_async_copy(src, dst, store.at[i]))
        outs[-1].start()

    ogp[...] = mm(errs[...], flat[...], NN).astype(BF16)
    write(0, ogp, grad_proj)
    ncol.unpack(nflat)
    for q in ORDER:
        inner[q].turn()
    gates.pass_on()
    gates.finish()
    ogg[...] = mm(ggs[0:448], nflat[...], NN).astype(BF16)
    write(2, ogg, grad_gate)
    ogu[...] = mm(ggs[448:896], nflat[...], NN).astype(BF16)
    write(3, ogu, grad_up)
    bcol.plane.finish()
    bcol.unpack(flat)
    hiddens.finish()
    ogd[...] = mm(hids[...], flat[...], NN).astype(BF16)
    write(4, ogd, grad_down)
    stats.wait_recv()
    whole = (statz[0] + statz[1] + statz[2] + statz[3]) / 4096.0
    stat[...] = jnp.broadcast_to(whole[0:1], (128, 128)).T
    for q in ORDER:
        v = inner[q].finish()
        r = rows_of(q)
        scale = jnp.concatenate([invs[r, :], invs[r, :]], axis=1)
        mean = jnp.concatenate([stat[r, :], stat[r, :]], axis=1)
        scaled = v * gain[:, share_at]
        oig[r, :] = fgrad[r, :] + scale * (scaled - up(xin[r, share_at]) * scale * mean)
    write(1, oig, input_grad)
    bcol.wait_first()
    for copy in net.copies:
        copy.wait_send()
    for copy in outs:
        copy.wait()


def move(*refs):
    srcs, dsts, held = refs[0:5], refs[5:10], refs[10:15]
    came, went = refs[15], refs[16]
    ins = [pltpu.make_async_copy(s, h, came.at[i]) for i, (s, h) in enumerate(zip(srcs, held))]
    outs = [pltpu.make_async_copy(h, d, went.at[i]) for i, (h, d) in enumerate(zip(held, dsts))]
    for copy in ins:
        copy.start()
    for i, copy in zip(ins, outs):
        i.wait()
        copy.start()
    for copy in outs:
        copy.wait()


def shards(
    student_in,
    norm_gain,
    gate_weight,
    up_weight,
    down_weight,
    projection,
    teacher_in,
    teacher_gate,
    teacher_up,
    teacher_down,
):
    vmem = pltpu.VMEM
    anyspec = pl.BlockSpec(memory_space=pl.ANY)
    shapes = (
        jax.ShapeDtypeStruct((448, 512), BF16),
        jax.ShapeDtypeStruct((448, 512), BF16),
        jax.ShapeDtypeStruct((448, 512), BF16),
        jax.ShapeDtypeStruct((512, 512), BF16),
        jax.ShapeDtypeStruct((128, 256), F32),
    )
    made = pl.pallas_call(
        kernel,
        out_shape=shapes,
        in_specs=[anyspec] * 10,
        out_specs=(anyspec,) * 5,
        scratch_shapes=[
            vmem((128, 4096), BF16),
            vmem((1, 4096), F32),
            vmem((448, 4096), BF16),
            vmem((448, 4096), BF16),
            vmem((448, 4096), BF16),
            vmem((512, 4096), BF16),
            vmem((1024, 1024), BF16),
            vmem((1024, 896), BF16),
            vmem((1024, 896), BF16),
            vmem((896, 1024), BF16),
            vmem((1024, 896), BF16),
            vmem((4, 2, 128, 1792), BF16),
            vmem((4, 128, 1792), BF16),
            vmem((6, 64, 1792), BF16),
            vmem((896, 1024), BF16),
            vmem((4, 4, 4, 128, 128), BF16),
            vmem((4, 3, 4, 128, 128), BF16),
            vmem((4, 4, 128, 128), BF16),
            vmem((4, 3, 128, 128), BF16),
            vmem((3, 4, 4, 4, 32, 256), BF16),
            vmem((3, 4, 3, 4, 32, 256), BF16),
            vmem((3, 4, 4, 32, 256), BF16),
            vmem((3, 4, 3, 32, 256), BF16),
            vmem((4, 4, 4, 32, 256), BF16),
            vmem((4, 4, 4, 32, 256), BF16),
            vmem((4, 4, 4, 32, 256), BF16),
            vmem((8, 2, 4, 32, 256), BF16),
            vmem((8, 2, 4, 32, 256), BF16),
            vmem((4, 4, 4, 32, 256), BF16),
            vmem((1024, 512), BF16),
            vmem((1024, 512), BF16),
            vmem((448, 1024), BF16),
            vmem((512, 1024), BF16),
            vmem((896, 1024), BF16),
            vmem((448, 128), F32),
            vmem((448, 128), F32),
            vmem((448, 128), F32),
            vmem((512, 128), F32),
            vmem((448, 128), F32),
            vmem((4, 128, 128), BF16),
            vmem((512, 128), BF16),
            vmem((128, 256), F32),
            vmem((128, 128), F32),
            vmem((4, 8, 128), F32),
            vmem((4, 8, 128), F32),
            vmem((128, 128), F32),
            vmem((448, 512), BF16),
            vmem((448, 512), BF16),
            vmem((448, 512), BF16),
            vmem((512, 512), BF16),
            vmem((128, 256), F32),
            pltpu.SemaphoreType.DMA((13,)),
            pltpu.SemaphoreType.DMA((5,)),
            pltpu.SemaphoreType.DMA((SEMS,)),
            pltpu.SemaphoreType.DMA((SEMS,)),
        ],
        compiler_params=pltpu.CompilerParams(
            collective_id=0, has_side_effects=True, vmem_limit_bytes=67043328
        ),
    )(
        student_in,
        norm_gain.reshape(1, -1),
        gate_weight.T,
        up_weight.T,
        down_weight,
        projection.transpose(1, 2, 0).reshape(512, -1),
        teacher_in,
        teacher_gate,
        teacher_up,
        teacher_down,
    )
    gg, gu, gd, gp, ig = pl.pallas_call(
        move,
        out_shape=shapes,
        in_specs=[anyspec] * 5,
        out_specs=(anyspec,) * 5,
        scratch_shapes=[vmem(s.shape, s.dtype) for s in shapes]
        + [pltpu.SemaphoreType.DMA((5,)), pltpu.SemaphoreType.DMA((5,))],
    )(*made)
    return gg.T, gu.T, gd, gp.reshape(8, 64, 512).transpose(2, 0, 1), ig


def solution(mesh):
    split = Mesh(mesh.devices.reshape(2, 4, 2, 2, 4), ("zh", "y", "c", "zl", "x"))
    in_specs = (
        P(WID, None),
        P(),
        P(None, GH),
        P(None, GH),
        P(GH, None),
        P(None, None, GH),
        P(None, WID),
        P(WID, GH),
        P(WID, GH),
        P(GH, WID),
    )
    out_specs = (
        P(WID, GH),
        P(WID, GH),
        P(GH, WID),
        P(WID, None, GH),
        P(WID, GH),
    )
    return jax.shard_map(
        shards, mesh=split, in_specs=in_specs, out_specs=out_specs, check_vma=False
    )
```

```python
import jax
import jax.numpy as jnp
from jax import lax
from jax.experimental import pallas as pl
from jax.experimental.pallas import tpu as pltpu
from jax.sharding import Mesh
from jax.sharding import PartitionSpec as P

MESH = pl.DeviceIdType.MESH
F32 = jnp.float32
BF16 = jnp.bfloat16
WID = ("y", "c")
GH = ("zh", "zl", "x")
SEMS = 101
ORDER = (0, 2, 1, 3)

NN = (((1,), (0,)), ((), ()))
NT = (((1,), (1,)), ((), ()))
TN = (((0,), (0,)), ((), ()))


def mm(a, b, dims):
    return lax.dot_general(a, b, dims, preferred_element_type=F32)


def up(v):
    return v.astype(F32)


def mod4(v):
    return lax.rem(v, 4)


class Net:
    def __init__(self, send, recv):
        zh, y, c, zl, x = [lax.axis_index(a) for a in ("zh", "y", "c", "zl", "x")]
        self.z, self.x, self.y, self.c = zh * 2 + zl, x, y, c
        self.send, self.recv, self.copies, self.count = send, recv, [], 0

    def at(self, z=None, x=None, y=None, c=None):
        z = self.z if z is None else z
        return {
            "zh": lax.div(z, 2),
            "zl": lax.rem(z, 2),
            "x": self.x if x is None else x,
            "y": self.y if y is None else y,
            "c": self.c if c is None else c,
        }

    def along(self, axis, offset):
        return self.at(**{axis: mod4(getattr(self, axis) + offset)})

    def make(self, src, dst, peer, i):
        return pltpu.make_async_remote_copy(
            src_ref=src,
            dst_ref=dst,
            send_sem=self.send.at[i],
            recv_sem=self.recv.at[i],
            device_id=peer,
            device_id_type=MESH,
        )

    def slots(self, n):
        self.count += n
        return self.count - n

    def put(self, src, dst, peer):
        copy = self.make(src, dst, peer, self.slots(1))
        copy.start()
        self.copies.append(copy)
        return copy

    def group(self, size):
        whole = self.make(size, size, self.at(c=1 - self.c), self.slots(1))
        self.copies.append(whole)
        return Group(self, whole, self.count - 1)


class Group:
    def __init__(self, net, whole, i):
        self.net, self.whole, self.i = net, whole, i

    def put(self, src, dst, peer):
        self.net.make(src, dst, peer, self.i).start()

    def wait_recv(self):
        self.whole.wait_recv()


class RingSum:
    def __init__(self, net, axis, src, buf):
        self.net, self.axis, self.src, self.buf = net, axis, src, buf
        me = getattr(net, axis)
        self.me, self.r, self.o, self.l = me, mod4(me + 1), mod4(me + 2), mod4(me + 3)
        self.right, self.left = net.along(axis, 1), net.along(axis, 3)

    def far(self):
        self.m1 = self.net.put(self.src(self.o, 0), self.buf.at[0], self.right)
        self.n1 = self.net.put(self.src(self.o, 1), self.buf.at[1], self.left)

    def near_r(self):
        self.m2 = self.net.put(self.src(self.r, 1), self.buf.at[2], self.right)

    def near_l(self):
        self.n2 = self.net.put(self.src(self.l, 0), self.buf.at[3], self.left)

    def start(self):
        self.far()
        self.near_r()
        self.near_l()

    def relay(self):
        buf = self.buf
        self.m1.wait_recv()
        buf[0] = (up(buf[0]) + up(self.src(self.r, 0)[...])).astype(BF16)
        self.m3 = self.net.put(buf.at[0], buf.at[4], self.right)
        self.n1.wait_recv()
        buf[1] = (up(buf[1]) + up(self.src(self.l, 1)[...])).astype(BF16)
        self.n3 = self.net.put(buf.at[1], buf.at[5], self.left)

    def finish(self):
        buf = self.buf
        self.n2.wait_recv()
        self.m3.wait_recv()
        first = up(self.src(self.me, 0)[...]) + up(buf[3]) + up(buf[4])
        self.m2.wait_recv()
        self.n3.wait_recv()
        second = up(self.src(self.me, 1)[...]) + up(buf[2]) + up(buf[5])
        return first, second


class PlaneSum:
    def __init__(self, net, axes, src, buf1, mid, buf2):
        self.net, self.axes, self.src = net, axes, src
        self.buf1, self.mid, self.buf2 = buf1, mid, buf2

    def deal(self, axis, src, buf):
        me = getattr(self.net, axis)
        group = self.net.group(buf)
        for o in (2, 1, 3):
            group.put(src(mod4(me + o)), buf.at[o - 1], self.net.along(axis, o))
        return group

    def total(self, group, own, buf):
        group.wait_recv()
        return up(own[...]) + up(buf[0]) + up(buf[1]) + up(buf[2])

    def start(self):
        self.one = self.deal(self.axes[0], self.src, self.buf1)

    def turn(self):
        me = getattr(self.net, self.axes[0])
        self.mid[...] = self.total(self.one, self.src(me), self.buf1).astype(BF16)
        self.second()

    def second(self):
        self.two = self.deal(self.axes[1], lambda d: self.mid.at[d], self.buf2)

    def finish(self):
        me = getattr(self.net, self.axes[1])
        return self.total(self.two, self.mid.at[me], self.buf2)


class PlaneAll:
    def __init__(self, net, data, sizes):
        self.net, self.data, self.sizes, self.groups = net, data, sizes, {}

    def copies(self, q, piece, axis, size):
        group = self.groups[q] = self.net.group(size)
        for o in (2, 1, 3):
            group.put(piece, piece, self.net.along(axis, o))

    def start(self, *blocks):
        for q in blocks:
            piece = self.data.at[self.net.z, self.net.x, q]
            self.copies(q, piece, "z" if q < 2 else "x", self.sizes[0])

    def turn(self, *blocks):
        for q in blocks:
            self.groups[q].wait_recv()
            if q < 2:
                self.copies(q, self.data.at[:, self.net.x, q], "x", self.sizes[1])
            else:
                self.copies(q, self.data.at[self.net.z, :, q], "z", self.sizes[1])

    def finish(self):
        for q in ORDER:
            self.groups[q].wait_recv()

    def ring_parts(self):
        net, data = self.net, self.data
        return (
            ("x", lambda d: data.at[:, d, pl.ds(0, 2)], lambda d, h: data.at[:, d, h]),
            ("z", lambda d: data.at[d, :, pl.ds(2, 2)], lambda d, h: data.at[d, :, 2 + h]),
        )

    def ring_turn(self):
        net, self.near = self.net, []
        for i, (axis, whole, _) in enumerate(self.ring_parts()):
            for q in (2 * i, 2 * i + 1):
                self.groups[q].wait_recv()
            own = whole(getattr(net, axis))
            self.near += [net.put(own, own, net.along(axis, o)) for o in (1, 3)]

    def ring_relay(self):
        net, self.far = self.net, []
        for i, (axis, _, part) in enumerate(self.ring_parts()):
            me = getattr(net, axis)
            for j, (o, h) in enumerate(((1, 0), (3, 1))):
                self.near[2 * i + j].wait_recv()
                piece = part(mod4(me + 4 - o), h)
                self.far.append(net.put(piece, piece, net.along(axis, o)))

    def ring_finish(self):
        for copy in self.far:
            copy.wait_recv()


class TokenDirect:
    def __init__(self, net, data):
        self.net, self.data = net, data
        self.own = self.slot(0)

    def slot(self, o):
        at = pl.multiple_of((mod4(self.net.y + o) * 2 + self.net.c) * 128, 128)
        return self.data.at[:, pl.ds(at, 128)]

    def start(self):
        net, own = self.net, self.own
        self.mate = net.at(c=1 - net.c)
        self.far = net.group(self.data.at[:, pl.ds(0, 384)])
        self.near = net.group(self.data.at[:, pl.ds(0, 512)])
        for o in (2, 1, 3):
            self.far.put(own, own, net.along("y", o))
        self.near.put(own, own, self.mate)

    def pass_on(self):
        self.far.wait_recv()
        for o in (2, 1, 3):
            piece = self.slot(o)
            self.near.put(piece, piece, self.mate)

    def finish(self):
        self.near.wait_recv()


class TokenAll:
    def __init__(self, net, data):
        self.net, self.data, self.rows = net, data, data.shape[0]
        self.own = self.slot(0)
        self.mate = net.at(c=1 - net.c)
        self.mates = {}

    def slot(self, o, h=None):
        at = pl.multiple_of((mod4(self.net.y + o) * 2 + self.net.c) * 128, 128)
        if h is None:
            return self.data.at[:, pl.ds(at, 128)]
        half = self.rows // 2
        return self.data.at[pl.ds(h * half, half), pl.ds(at, 128)]

    def send(self, o, h, to):
        piece = self.slot(o, h)
        return self.net.put(piece, piece, self.net.along("y", to))

    def share(self, o):
        piece = self.slot(o)
        self.mates[o] = self.net.put(piece, piece, self.mate)

    def start(self):
        self.share(0)
        self.r0, self.l1 = self.send(0, 0, 1), self.send(0, 1, 3)
        self.r1, self.l0 = self.send(0, 1, 1), self.send(0, 0, 3)

    def relay(self):
        self.r0.wait_recv()
        self.rr = self.send(3, 0, 1)
        self.l1.wait_recv()
        self.ll = self.send(1, 1, 3)

    def near(self):
        self.l0.wait_recv()
        self.share(1)
        self.r1.wait_recv()
        self.share(3)

    def finish(self):
        self.rr.wait_recv()
        self.ll.wait_recv()
        self.share(2)

    def wait(self, o):
        self.mates[o].wait_recv()


class Direct:
    def __init__(self, net, source, data):
        self.net, self.source, self.data = net, source, data

        self.group = net.group(data.at[pl.ds(0, 7)])

    def start(self, offsets):
        net = self.net
        to = self.data.at[net.y * 2 + net.c]
        if 0 in offsets:
            to[...] = self.source[net.y, pl.ds(2 * net.c, 2)]
        for o in offsets:
            for flip in (0, 1):
                if o or flip:
                    y, c = mod4(net.y + o), lax.rem(net.c + flip, 2)
                    piece = self.source.at[y, pl.ds(2 * c, 2)]
                    self.group.put(piece, to, net.at(y=y, c=c))

    def unpack(self, out):
        self.group.wait_recv()

        def body(w, _):
            rows = pl.ds(pl.multiple_of(w * 128, 128), 128)
            for half in (0, 1):
                out[rows, 256 * half : 256 * half + 256] = self.data[w, half].reshape(128, 256)
            return 0

        lax.fori_loop(0, 8, body, 0)


class Columns:
    def __init__(self, net, source, data, sizes):
        self.net, self.source, self.data = net, source, data
        self.plane = PlaneAll(net, data, sizes)

    def spread(self):
        net = self.net
        w, half = net.y * 2 + net.c, lax.div(net.x, 2)
        self.base, self.w = net.slots(8), w
        self.sent = []
        self.alone = jnp.logical_and(net.y == net.z, net.c == half)
        for o in range(4):
            for i in (0, 1):
                z, x = mod4(net.z + o), mod4(net.x + 2 * i)
                rows = pl.ds(pl.multiple_of(lax.div(x, 2) * 16, 16), 16)
                piece = self.source.at[net.z, net.x, z, rows]
                to = self.data.at[z, x, net.y, pl.ds(pl.multiple_of(net.c * 16, 16), 16)]
                copy = pltpu.make_async_remote_copy(
                    src_ref=piece,
                    dst_ref=to,
                    send_sem=net.send.at[self.base + 2 * o + i],
                    recv_sem=net.recv.at[self.base + w],
                    device_id=net.at(z=z, x=x, y=net.z, c=half),
                    device_id_type=MESH,
                )
                self.sent.append(copy)
                if o or i:
                    copy.start()
                    net.copies.append(copy)
                else:
                    here = (piece, to)
        first, (piece, to) = self.sent[0], here

        @pl.when(self.alone)
        def _():
            to[...] = piece[...]

        @pl.when(jnp.logical_not(self.alone))
        def _():
            first.start()

    def wait_first(self):
        @pl.when(jnp.logical_not(self.alone))
        def _():
            self.sent[0].wait_send()

    def start(self):
        net = self.net
        for w in range(8):
            slot = self.data.at[net.z, net.x, w // 2, pl.ds(16 * (w % 2), 16)]
            copy = net.make(slot, slot, net.at(c=1 - net.c), self.base + w)

            @pl.when(jnp.logical_not(jnp.logical_and(self.alone, self.w == w)))
            def _():
                copy.wait_recv()

        self.plane.start(*ORDER)

    def unpack(self, out):
        data = self.data

        def body(y, _):
            for c in (0, 1):
                for half in (0, 1):
                    parts = [
                        data[z, 2 * i + half, y, 16 * c : 16 * c + 16]
                        for z in range(4)
                        for i in (0, 1)
                    ]
                    at = pl.multiple_of(y * 256 + c * 128, 128)
                    out[pl.ds(at, 128), 256 * half : 256 * half + 256] = jnp.concatenate(
                        parts, axis=0
                    )
            return 0

        lax.fori_loop(0, 4, body, 0)


def share_of(ref, z, x):
    return ref[z, x].reshape(128, 256)


def wide_of(ref, z):
    return jnp.concatenate([share_of(ref, z, x) for x in range(4)], axis=1)


def kernel(
    student_in,
    norm_gain,
    gate_weight,
    up_weight,
    down_weight,
    projection,
    teacher_in,
    teacher_gate,
    teacher_up,
    teacher_down,
    grad_gate,
    grad_up,
    grad_down,
    grad_proj,
    input_grad,
    xin,
    gain,
    wg,
    wu,
    wd,
    pj,
    tin,
    tg,
    tu,
    td,
    tdt,
    parts,
    mate,
    ring,
    thid,
    feat,
    feat1,
    featm,
    feat2,
    sums,
    sums1,
    summ,
    sums2,
    normed,
    summed,
    bgrad,
    ncols,
    scols,
    bcols,
    flat,
    nflat,
    hids,
    errs,
    ggs,
    gate,
    upsum,
    sigma,
    acc,
    acc2,
    tshare,
    target,
    fgrad,
    stat,
    statx,
    statz,
    invs,
    ogg,
    ogu,
    ogd,
    ogp,
    oig,
    load,
    store,
    send,
    recv,
):
    net = Net(send, recv)
    z, x, y, c = net.z, net.x, net.y, net.c
    ys = [mod4(y + o) for o in range(4)]

    rows_in = [pl.ds(pl.multiple_of(d * 256, 256), 256) for d in ys]
    loads = {}
    for i, (name, src, dst) in enumerate(
        (
            (2, teacher_in.at[rows_in[2]], tin.at[rows_in[2]]),
            ("tg", teacher_gate, tg),
            ("tu", teacher_up, tu),
            (1, teacher_in.at[rows_in[1]], tin.at[rows_in[1]]),
            (3, teacher_in.at[rows_in[3]], tin.at[rows_in[3]]),
            (0, teacher_in.at[rows_in[0]], tin.at[rows_in[0]]),
            ("xin", student_in, xin),
            ("gain", norm_gain, gain),
            ("wg", gate_weight, wg),
            ("wu", up_weight, wu),
            ("wd", down_weight, wd),
            ("td", teacher_down, td),
            ("pj", projection, pj),
        )
    ):
        loads[name] = pltpu.make_async_copy(src, dst, load.at[i])
        loads[name].start()

    barrier = pltpu.get_barrier_semaphore()
    peers = [net.at(y=mod4(y + o), c=lax.rem(c + f, 2)) for o in range(4) for f in (0, 1) if o or f]
    peers += [net.along("x", o) for o in (1, 2, 3)] + [net.along("z", o) for o in (1, 2, 3)]
    for peer in peers:
        pl.semaphore_signal(barrier, inc=1, device_id=peer, device_id_type=MESH)
    near = 2 * c + lax.rem(x, 2)
    for o in range(4):
        for f in (0, 1):
            source = net.at(z=y, x=near, y=mod4(y + o), c=lax.rem(c + f, 2))
            if o or f:
                pl.semaphore_signal(barrier, inc=1, device_id=source, device_id_type=MESH)
            else:

                @pl.when(jnp.logical_or(z != y, x != near))
                def _():
                    pl.semaphore_signal(barrier, inc=1, device_id=source, device_id_type=MESH)

    tsum = RingSum(
        net, "y", lambda d, h: parts.at[d, c, pl.ds(64 * h, 64)], ring
    )
    pair = {}

    def project(o):
        d = ys[o]
        loads[o].wait()
        rows = tin[rows_in[o], :]
        if o == 2:
            loads["tg"].wait()
        parts[d, :, :, 0:896] = mm(rows, tg[...], NN).astype(BF16).reshape(2, 128, 896)
        if o == 2:
            loads["tu"].wait()
        parts[d, :, :, 896:1792] = mm(rows, tu[...], NN).astype(BF16).reshape(2, 128, 896)

    def swap(o):
        d = ys[o]
        pair[o] = net.put(parts.at[d, 1 - c], mate.at[d], net.at(c=1 - c))

    def join(o):
        d = ys[o]
        pair[o].wait_recv()
        parts[d, c] = (up(parts[d, c]) + up(mate[d])).astype(BF16)

    project(2)
    own = jnp.logical_and(y == z, c == lax.div(x, 2)).astype(jnp.int32)
    pl.semaphore_wait(barrier, len(peers) + 8 - own)
    swap(2)
    project(1)
    swap(1)
    join(2)
    tsum.far()
    project(3)
    swap(3)
    join(1)
    tsum.near_r()

    loads["xin"].wait()
    loads["gain"].wait()

    def squares(b, total):
        v = up(xin[:, pl.ds(pl.multiple_of(b * 256, 256), 256)])
        return total + v * v

    total = lax.fori_loop(0, 16, squares, jnp.zeros((128, 256), F32))
    inv = lax.rsqrt(jnp.sum(total, axis=1, keepdims=True) / 4096.0 + 1e-05)
    invs[...] = jnp.broadcast_to(inv, (128, 128))

    def norm(b, _):
        at = pl.ds(pl.multiple_of(b * 256, 256), 256)
        scale = jnp.concatenate([invs[...], invs[...]], axis=1)
        v = up(xin[:, at]) * scale * gain[:, at]
        normed[lax.div(b, 4), lax.rem(b, 4)] = v.astype(BF16).reshape(4, 32, 256)
        return 0

    lax.fori_loop(0, 16, norm, 0)

    for name in ("wg", "wu", "wd"):
        loads[name].wait()

    def students(first, second, source, out_first, out_second):
        def body(b, _):
            at = pl.ds(pl.multiple_of(b * 1024, 1024), 1024)
            wide = wide_of(source, b)
            out_first[...] += mm(first[:, at], wide, NT)
            if second is not None:
                out_second[...] += mm(second[:, at], wide, NT)
            return 0

        out_first[...] = jnp.zeros(out_first.shape, F32)
        if second is not None:
            out_second[...] = jnp.zeros(out_second.shape, F32)
        lax.fori_loop(0, 4, body, 0)

    def back(out, pairs):
        def body(b, _):
            at = pl.ds(pl.multiple_of(b * 1024, 1024), 1024)
            v = sum(mm(small, w[:, at], TN) for small, w in pairs).astype(BF16)
            for i in range(4):
                out[b, i] = v[:, 256 * i : 256 * i + 256].reshape(4, 32, 256)
            return 0

        lax.fori_loop(0, 4, body, 0)

    def plane_sums(n):
        data = sums.at[n]

        def block(q):
            if q < 2:
                axes, src = ("x", "z"), lambda d: data.at[:, d, q]
            else:
                axes, src = ("z", "x"), lambda d: data.at[d, :, q]
            return PlaneSum(net, axes, src, sums1.at[n, q], summ.at[n, q], sums2.at[n, q])

        return [block(q) for q in range(4)]

    students(wg, wu, normed, gate, upsum)
    join(3)
    tsum.near_l()
    sig = jax.nn.sigmoid(gate[...])
    sigma[...] = sig
    hid = (gate[...] * sig * upsum[...]).astype(BF16)
    hiddens = TokenDirect(net, hids)
    hiddens.own[...] = hid
    back(sums.at[0], ((hid, wd),))
    branch = plane_sums(0)
    for q in ORDER:
        branch[q].start()
    tsum.relay()
    project(0)
    swap(0)
    loads["td"].wait()
    tdt[...] = td[...].T
    join(0)
    for q in ORDER:
        branch[q].turn()

    first, second = tsum.finish()
    sums_all = jnp.concatenate([first, second], axis=0)
    g = sums_all[:, :896]
    teach = g * jax.nn.sigmoid(g) * sums_all[:, 896:]
    teachers = TokenAll(net, thid)
    teachers.own[...] = teach.T.astype(BF16)
    teachers.start()

    order = [ys[0], ys[1], ys[3], ys[2]]

    def group(k):
        d = order[k]
        if k % 2 == 0:
            axes, src = ("x", "z"), lambda e: feat.at[:, e, d]
        else:
            axes, src = ("z", "x"), lambda e: feat.at[e, :, d]
        return PlaneSum(net, axes, src, feat1.at[k], featm.at[k], feat2.at[k])

    teaching = [group(k) for k in range(4)]

    def feature(k, o):
        d = ys[o]
        teachers.wait(o)
        v = mm(tdt[...], thid[:, pl.ds(pl.multiple_of(d * 256, 256), 256)], NN).astype(BF16)
        for f in (0, 1):
            feat[:, :, d, 64 * f : 64 * f + 64] = v[:, 128 * f : 128 * f + 128].reshape(
                4, 4, 64, 128
            )
        teaching[k].start()

    rows_of = lambda q: pl.ds(32 * q, 32)
    share_at = pl.ds(pl.multiple_of((z * 4 + x) * 256, 256), 256)
    sizes = (sums2.at[0, 0], sums1.at[0, 0])
    sum_all = PlaneAll(net, summed, sizes)
    for q in ORDER:
        v = branch[q].finish()
        summed[z, x, q] = (up(xin[rows_of(q), share_at]) + v).astype(BF16)
        sum_all.start(q)
    feature(0, 0)
    teachers.relay()
    sum_all.ring_turn()
    teachers.near()
    feature(1, 1)
    teachers.finish()
    feature(2, 3)
    teaching[0].turn()
    feature(3, 2)
    sum_all.ring_relay()
    ncol = Direct(net, normed, ncols)
    ncol.start((2, 1, 3, 0))
    sent = net.group(target.at[pl.ds(0, 448)])

    def hand(k, v):
        d = order[k]
        tshare[d] = v.astype(BF16)
        to = target.at[pl.ds(pl.multiple_of((y * 2 + c) * 64, 64), 64)]
        for f in (0, 1):
            cc = lax.rem(c + f, 2)
            piece = tshare.at[d, pl.ds(pl.multiple_of(cc * 64, 64), 64)]
            if k == 0 and f == 0:
                to[...] = piece[...]
            else:
                sent.put(piece, to, net.at(y=d, c=cc))

    teaching[1].turn()
    teaching[2].turn()
    teaching[3].turn()
    sum_all.ring_finish()
    loads["pj"].wait()
    students(pj, None, summed, acc, None)
    for k in range(4):
        hand(k, teaching[k].finish())
    sent.wait_recv()

    err = ((acc[...] - up(target[...])) * (1.0 / 32.0)).astype(BF16)
    errors = TokenDirect(net, errs)
    errors.own[...] = err
    errors.start()
    back(sums.at[1], ((err, pj),))
    grads = plane_sums(1)
    for q in ORDER:
        grads[q].start()
    scol = Direct(net, summed, scols)
    scol.start((2, 0))
    for q in ORDER:
        grads[q].turn()
    grad_all = PlaneAll(net, bgrad, sizes)
    for q in ORDER:
        v = grads[q].finish()
        bgrad[z, x, q] = v.astype(BF16)
        grad_all.start(q)
        fgrad[rows_of(q), :] = v
    bcol = Columns(net, bgrad, bcols, sizes)
    bcol.spread()
    grad_all.turn(0, 2)
    errors.pass_on()
    scol.start((1, 3))
    hiddens.start()
    grad_all.turn(1, 3)
    errors.finish()
    bcol.start()
    grad_all.finish()

    students(wd, None, bgrad, acc2, None)
    hg = acc2[...]
    g, s = gate[...], sigma[...]
    gg = (hg * upsum[...] * s * (1.0 + g * (1.0 - s))).astype(BF16)
    ug = (hg * g * s).astype(BF16)
    moment = jnp.sum(up(gg) * g + up(ug) * upsum[...], axis=0, keepdims=True)
    gates = [TokenDirect(net, ggs.at[pl.ds(448 * i, 448)]) for i in (0, 1)]
    own_at = pl.ds(pl.multiple_of((y * 2 + c) * 128, 128), 128)
    ggs[0:448, own_at] = gg
    ggs[448:896, own_at] = ug
    gates[0].start()
    gates[1].start()

    def tell(ref, me, axis):
        group = net.group(ref.at[pl.ds(0, 3)])
        for o in (2, 1, 3):
            group.put(ref.at[me], ref.at[me], net.along(axis, o))
        return group

    statx[x] = jnp.broadcast_to(moment, (8, 128))
    stats = tell(statx, x, "x")
    bcol.plane.turn(0, 2)
    back(sums.at[2], ((gg, wg), (ug, wu)))
    inner = plane_sums(2)
    for q in ORDER:
        inner[q].start()
    bcol.plane.turn(1, 3)
    stats.wait_recv()
    statz[z] = statx[0] + statx[1] + statx[2] + statx[3]
    stats = tell(statz, z, "z")
    hiddens.pass_on()
    scol.unpack(flat)

    outs = []

    def write(i, src, dst):
        outs.append(pltpu.make_async_copy(src, dst, store.at[i]))
        outs[-1].start()

    ogp[...] = mm(errs[...], flat[...], NN).astype(BF16)
    write(0, ogp, grad_proj)
    ncol.unpack(nflat)
    gates[0].pass_on()
    for q in ORDER:
        inner[q].turn()
    gates[0].finish()
    ogg[...] = mm(ggs[0:448], nflat[...], NN).astype(BF16)
    write(2, ogg, grad_gate)
    gates[1].pass_on()
    gates[1].finish()
    ogu[...] = mm(ggs[448:896], nflat[...], NN).astype(BF16)
    write(3, ogu, grad_up)
    bcol.plane.finish()
    bcol.unpack(flat)
    hiddens.finish()
    ogd[...] = mm(hids[...], flat[...], NN).astype(BF16)
    write(4, ogd, grad_down)
    stats.wait_recv()
    whole = (statz[0] + statz[1] + statz[2] + statz[3]) / 4096.0
    stat[...] = jnp.broadcast_to(whole[0:1], (128, 128)).T
    for q in ORDER:
        v = inner[q].finish()
        r = rows_of(q)
        scale = jnp.concatenate([invs[r, :], invs[r, :]], axis=1)
        mean = jnp.concatenate([stat[r, :], stat[r, :]], axis=1)
        scaled = v * gain[:, share_at]
        oig[r, :] = fgrad[r, :] + scale * (scaled - up(xin[r, share_at]) * scale * mean)
    write(1, oig, input_grad)
    bcol.wait_first()
    for copy in net.copies:
        copy.wait_send()
    for copy in outs:
        copy.wait()


def move(*refs):
    srcs, dsts, held = refs[0:5], refs[5:10], refs[10:15]
    came, went = refs[15], refs[16]
    ins = [pltpu.make_async_copy(s, h, came.at[i]) for i, (s, h) in enumerate(zip(srcs, held))]
    outs = [pltpu.make_async_copy(h, d, went.at[i]) for i, (h, d) in enumerate(zip(held, dsts))]
    for copy in ins:
        copy.start()
    for i, copy in zip(ins, outs):
        i.wait()
        copy.start()
    for copy in outs:
        copy.wait()


def shards(
    student_in,
    norm_gain,
    gate_weight,
    up_weight,
    down_weight,
    projection,
    teacher_in,
    teacher_gate,
    teacher_up,
    teacher_down,
):
    vmem = pltpu.VMEM
    anyspec = pl.BlockSpec(memory_space=pl.ANY)
    shapes = (
        jax.ShapeDtypeStruct((448, 512), BF16),
        jax.ShapeDtypeStruct((448, 512), BF16),
        jax.ShapeDtypeStruct((448, 512), BF16),
        jax.ShapeDtypeStruct((512, 512), BF16),
        jax.ShapeDtypeStruct((128, 256), F32),
    )
    made = pl.pallas_call(
        kernel,
        out_shape=shapes,
        in_specs=[anyspec] * 10,
        out_specs=(anyspec,) * 5,
        scratch_shapes=[
            vmem((128, 4096), BF16),
            vmem((1, 4096), F32),
            vmem((448, 4096), BF16),
            vmem((448, 4096), BF16),
            vmem((448, 4096), BF16),
            vmem((512, 4096), BF16),
            vmem((1024, 1024), BF16),
            vmem((1024, 896), BF16),
            vmem((1024, 896), BF16),
            vmem((896, 1024), BF16),
            vmem((1024, 896), BF16),
            vmem((4, 2, 128, 1792), BF16),
            vmem((4, 128, 1792), BF16),
            vmem((6, 64, 1792), BF16),
            vmem((896, 1024), BF16),
            vmem((4, 4, 4, 128, 128), BF16),
            vmem((4, 3, 4, 128, 128), BF16),
            vmem((4, 4, 128, 128), BF16),
            vmem((4, 3, 128, 128), BF16),
            vmem((3, 4, 4, 4, 32, 256), BF16),
            vmem((3, 4, 3, 4, 32, 256), BF16),
            vmem((3, 4, 4, 32, 256), BF16),
            vmem((3, 4, 3, 32, 256), BF16),
            vmem((4, 4, 4, 32, 256), BF16),
            vmem((4, 4, 4, 32, 256), BF16),
            vmem((4, 4, 4, 32, 256), BF16),
            vmem((8, 2, 4, 32, 256), BF16),
            vmem((8, 2, 4, 32, 256), BF16),
            vmem((4, 4, 4, 32, 256), BF16),
            vmem((1024, 512), BF16),
            vmem((1024, 512), BF16),
            vmem((448, 1024), BF16),
            vmem((512, 1024), BF16),
            vmem((896, 1024), BF16),
            vmem((448, 128), F32),
            vmem((448, 128), F32),
            vmem((448, 128), F32),
            vmem((512, 128), F32),
            vmem((448, 128), F32),
            vmem((4, 128, 128), BF16),
            vmem((512, 128), BF16),
            vmem((128, 256), F32),
            vmem((128, 128), F32),
            vmem((4, 8, 128), F32),
            vmem((4, 8, 128), F32),
            vmem((128, 128), F32),
            vmem((448, 512), BF16),
            vmem((448, 512), BF16),
            vmem((448, 512), BF16),
            vmem((512, 512), BF16),
            vmem((128, 256), F32),
            pltpu.SemaphoreType.DMA((13,)),
            pltpu.SemaphoreType.DMA((5,)),
            pltpu.SemaphoreType.DMA((SEMS,)),
            pltpu.SemaphoreType.DMA((SEMS,)),
        ],
        compiler_params=pltpu.CompilerParams(
            collective_id=0, has_side_effects=True, vmem_limit_bytes=67043328
        ),
    )(
        student_in,
        norm_gain.reshape(1, -1),
        gate_weight.T,
        up_weight.T,
        down_weight,
        projection.transpose(1, 2, 0).reshape(512, -1),
        teacher_in,
        teacher_gate,
        teacher_up,
        teacher_down,
    )
    gg, gu, gd, gp, ig = pl.pallas_call(
        move,
        out_shape=shapes,
        in_specs=[anyspec] * 5,
        out_specs=(anyspec,) * 5,
        scratch_shapes=[vmem(s.shape, s.dtype) for s in shapes]
        + [pltpu.SemaphoreType.DMA((5,)), pltpu.SemaphoreType.DMA((5,))],
    )(*made)
    return gg.T, gu.T, gd, gp.reshape(8, 64, 512).transpose(2, 0, 1), ig


def solution(mesh):
    split = Mesh(mesh.devices.reshape(2, 4, 2, 2, 4), ("zh", "y", "c", "zl", "x"))
    in_specs = (
        P(WID, None),
        P(),
        P(None, GH),
        P(None, GH),
        P(GH, None),
        P(None, None, GH),
        P(None, WID),
        P(WID, GH),
        P(WID, GH),
        P(GH, WID),
    )
    out_specs = (
        P(WID, GH),
        P(WID, GH),
        P(GH, WID),
        P(WID, None, GH),
        P(WID, GH),
    )
    return jax.shard_map(
        shards, mesh=split, in_specs=in_specs, out_specs=out_specs, check_vma=False
    )
```

```python
import jax
import jax.numpy as jnp
from jax import lax
from jax.experimental import pallas as pl
from jax.experimental.pallas import tpu as pltpu
from jax.sharding import Mesh
from jax.sharding import PartitionSpec as P

MESH = pl.DeviceIdType.MESH
F32 = jnp.float32
BF16 = jnp.bfloat16
WID = ("y", "c")
GH = ("zh", "zl", "x")
SEMS = 101
ORDER = (0, 2, 1, 3)

NN = (((1,), (0,)), ((), ()))
NT = (((1,), (1,)), ((), ()))
TN = (((0,), (0,)), ((), ()))


def mm(a, b, dims):
    return lax.dot_general(a, b, dims, preferred_element_type=F32)


def up(v):
    return v.astype(F32)


def mod4(v):
    return lax.rem(v, 4)


class Net:
    def __init__(self, send, recv):
        zh, y, c, zl, x = [lax.axis_index(a) for a in ("zh", "y", "c", "zl", "x")]
        self.z, self.x, self.y, self.c = zh * 2 + zl, x, y, c
        self.send, self.recv, self.copies, self.count = send, recv, [], 0

    def at(self, z=None, x=None, y=None, c=None):
        z = self.z if z is None else z
        return {
            "zh": lax.div(z, 2),
            "zl": lax.rem(z, 2),
            "x": self.x if x is None else x,
            "y": self.y if y is None else y,
            "c": self.c if c is None else c,
        }

    def along(self, axis, offset):
        return self.at(**{axis: mod4(getattr(self, axis) + offset)})

    def make(self, src, dst, peer, i):
        return pltpu.make_async_remote_copy(
            src_ref=src,
            dst_ref=dst,
            send_sem=self.send.at[i],
            recv_sem=self.recv.at[i],
            device_id=peer,
            device_id_type=MESH,
        )

    def slots(self, n):
        self.count += n
        return self.count - n

    def put(self, src, dst, peer):
        copy = self.make(src, dst, peer, self.slots(1))
        copy.start()
        self.copies.append(copy)
        return copy

    def group(self, size):
        whole = self.make(size, size, self.at(c=1 - self.c), self.slots(1))
        self.copies.append(whole)
        return Group(self, whole, self.count - 1)


class Group:
    def __init__(self, net, whole, i):
        self.net, self.whole, self.i = net, whole, i

    def put(self, src, dst, peer):
        self.net.make(src, dst, peer, self.i).start()

    def wait_recv(self):
        self.whole.wait_recv()


class RingSum:
    def __init__(self, net, axis, src, buf):
        self.net, self.axis, self.src, self.buf = net, axis, src, buf
        me = getattr(net, axis)
        self.me, self.r, self.o, self.l = me, mod4(me + 1), mod4(me + 2), mod4(me + 3)
        self.right, self.left = net.along(axis, 1), net.along(axis, 3)

    def far(self):
        self.m1 = self.net.put(self.src(self.o, 0), self.buf.at[0], self.right)
        self.n1 = self.net.put(self.src(self.o, 1), self.buf.at[1], self.left)

    def near_r(self):
        self.m2 = self.net.put(self.src(self.r, 1), self.buf.at[2], self.right)

    def near_l(self):
        self.n2 = self.net.put(self.src(self.l, 0), self.buf.at[3], self.left)

    def start(self):
        self.far()
        self.near_r()
        self.near_l()

    def relay(self):
        buf = self.buf
        self.m1.wait_recv()
        buf[0] = (up(buf[0]) + up(self.src(self.r, 0)[...])).astype(BF16)
        self.m3 = self.net.put(buf.at[0], buf.at[4], self.right)
        self.n1.wait_recv()
        buf[1] = (up(buf[1]) + up(self.src(self.l, 1)[...])).astype(BF16)
        self.n3 = self.net.put(buf.at[1], buf.at[5], self.left)

    def finish(self):
        buf = self.buf
        self.n2.wait_recv()
        self.m3.wait_recv()
        first = up(self.src(self.me, 0)[...]) + up(buf[3]) + up(buf[4])
        self.m2.wait_recv()
        self.n3.wait_recv()
        second = up(self.src(self.me, 1)[...]) + up(buf[2]) + up(buf[5])
        return first, second


class PlaneSum:
    def __init__(self, net, axes, src, buf1, mid, buf2):
        self.net, self.axes, self.src = net, axes, src
        self.buf1, self.mid, self.buf2 = buf1, mid, buf2

    def deal(self, axis, src, buf):
        me = getattr(self.net, axis)
        group = self.net.group(buf)
        for o in (2, 1, 3):
            group.put(src(mod4(me + o)), buf.at[o - 1], self.net.along(axis, o))
        return group

    def total(self, group, own, buf):
        group.wait_recv()
        return up(own[...]) + up(buf[0]) + up(buf[1]) + up(buf[2])

    def start(self):
        self.one = self.deal(self.axes[0], self.src, self.buf1)

    def turn(self):
        me = getattr(self.net, self.axes[0])
        self.mid[...] = self.total(self.one, self.src(me), self.buf1).astype(BF16)
        self.second()

    def second(self):
        self.two = self.deal(self.axes[1], lambda d: self.mid.at[d], self.buf2)

    def finish(self):
        me = getattr(self.net, self.axes[1])
        return self.total(self.two, self.mid.at[me], self.buf2)


class PlaneAll:
    def __init__(self, net, data, sizes):
        self.net, self.data, self.sizes, self.groups = net, data, sizes, {}

    def copies(self, q, piece, axis, size):
        group = self.groups[q] = self.net.group(size)
        for o in (2, 1, 3):
            group.put(piece, piece, self.net.along(axis, o))

    def start(self, *blocks):
        for q in blocks:
            piece = self.data.at[self.net.z, self.net.x, q]
            self.copies(q, piece, "z" if q < 2 else "x", self.sizes[0])

    def turn(self, *blocks):
        for q in blocks:
            self.groups[q].wait_recv()
            if q < 2:
                self.copies(q, self.data.at[:, self.net.x, q], "x", self.sizes[1])
            else:
                self.copies(q, self.data.at[self.net.z, :, q], "z", self.sizes[1])

    def finish(self):
        for q in ORDER:
            self.groups[q].wait_recv()

    def ring_parts(self):
        net, data = self.net, self.data
        return (
            ("x", lambda d: data.at[:, d, pl.ds(0, 2)], lambda d, h: data.at[:, d, h]),
            ("z", lambda d: data.at[d, :, pl.ds(2, 2)], lambda d, h: data.at[d, :, 2 + h]),
        )

    def ring_turn(self):
        net, self.near = self.net, []
        for i, (axis, whole, _) in enumerate(self.ring_parts()):
            for q in (2 * i, 2 * i + 1):
                self.groups[q].wait_recv()
            own = whole(getattr(net, axis))
            self.near += [net.put(own, own, net.along(axis, o)) for o in (1, 3)]

    def ring_relay(self):
        net, self.far = self.net, []
        for i, (axis, _, part) in enumerate(self.ring_parts()):
            me = getattr(net, axis)
            for j, (o, h) in enumerate(((1, 0), (3, 1))):
                self.near[2 * i + j].wait_recv()
                piece = part(mod4(me + 4 - o), h)
                self.far.append(net.put(piece, piece, net.along(axis, o)))

    def ring_finish(self):
        for copy in self.far:
            copy.wait_recv()


class TokenDirect:
    def __init__(self, net, data):
        self.net, self.data = net, data
        self.own = self.slot(0)

    def slot(self, o):
        at = pl.multiple_of((mod4(self.net.y + o) * 2 + self.net.c) * 128, 128)
        return self.data.at[:, pl.ds(at, 128)]

    def start(self):
        net, own = self.net, self.own
        self.mate = net.at(c=1 - net.c)
        self.far = net.group(self.data.at[:, pl.ds(0, 384)])
        self.near = net.group(self.data.at[:, pl.ds(0, 512)])
        for o in (2, 1, 3):
            self.far.put(own, own, net.along("y", o))
        self.near.put(own, own, self.mate)

    def pass_on(self):
        self.far.wait_recv()
        for o in (2, 1, 3):
            piece = self.slot(o)
            self.near.put(piece, piece, self.mate)

    def finish(self):
        self.near.wait_recv()


class TokenAll:
    def __init__(self, net, data):
        self.net, self.data, self.rows = net, data, data.shape[0]
        self.own = self.slot(0)
        self.mate = net.at(c=1 - net.c)
        self.mates = {}

    def slot(self, o, h=None):
        at = pl.multiple_of((mod4(self.net.y + o) * 2 + self.net.c) * 128, 128)
        if h is None:
            return self.data.at[:, pl.ds(at, 128)]
        half = self.rows // 2
        return self.data.at[pl.ds(h * half, half), pl.ds(at, 128)]

    def send(self, o, h, to):
        piece = self.slot(o, h)
        return self.net.put(piece, piece, self.net.along("y", to))

    def share(self, o):
        piece = self.slot(o)
        self.mates[o] = self.net.put(piece, piece, self.mate)

    def start(self):
        self.share(0)
        self.r0, self.l1 = self.send(0, 0, 1), self.send(0, 1, 3)
        self.r1, self.l0 = self.send(0, 1, 1), self.send(0, 0, 3)

    def relay(self):
        self.r0.wait_recv()
        self.rr = self.send(3, 0, 1)
        self.l1.wait_recv()
        self.ll = self.send(1, 1, 3)

    def near(self):
        self.l0.wait_recv()
        self.share(1)
        self.r1.wait_recv()
        self.share(3)

    def finish(self):
        self.rr.wait_recv()
        self.ll.wait_recv()
        self.share(2)

    def wait(self, o):
        self.mates[o].wait_recv()


class Direct:
    def __init__(self, net, source, data):
        self.net, self.source, self.data = net, source, data

        self.group = net.group(data.at[pl.ds(0, 7)])

    def start(self, offsets):
        net = self.net
        to = self.data.at[net.y * 2 + net.c]
        if 0 in offsets:
            to[...] = self.source[net.y, pl.ds(2 * net.c, 2)]
        for o in offsets:
            for flip in (0, 1):
                if o or flip:
                    y, c = mod4(net.y + o), lax.rem(net.c + flip, 2)
                    piece = self.source.at[y, pl.ds(2 * c, 2)]
                    self.group.put(piece, to, net.at(y=y, c=c))

    def unpack(self, out):
        self.group.wait_recv()

        def body(w, _):
            rows = pl.ds(pl.multiple_of(w * 128, 128), 128)
            for half in (0, 1):
                out[rows, 256 * half : 256 * half + 256] = self.data[w, half].reshape(128, 256)
            return 0

        lax.fori_loop(0, 8, body, 0)


class Columns:
    def __init__(self, net, source, data, sizes):
        self.net, self.source, self.data = net, source, data
        self.plane = PlaneAll(net, data, sizes)

    def spread(self):
        net = self.net
        w, half = net.y * 2 + net.c, lax.div(net.x, 2)
        self.base, self.w = net.slots(8), w
        self.sent = []
        self.alone = jnp.logical_and(net.y == net.z, net.c == half)
        for o in range(4):
            for i in (0, 1):
                z, x = mod4(net.z + o), mod4(net.x + 2 * i)
                rows = pl.ds(pl.multiple_of(lax.div(x, 2) * 16, 16), 16)
                piece = self.source.at[net.z, net.x, z, rows]
                to = self.data.at[z, x, net.y, pl.ds(pl.multiple_of(net.c * 16, 16), 16)]
                copy = pltpu.make_async_remote_copy(
                    src_ref=piece,
                    dst_ref=to,
                    send_sem=net.send.at[self.base + 2 * o + i],
                    recv_sem=net.recv.at[self.base + w],
                    device_id=net.at(z=z, x=x, y=net.z, c=half),
                    device_id_type=MESH,
                )
                self.sent.append(copy)
                if o or i:
                    copy.start()
                    net.copies.append(copy)
                else:
                    here = (piece, to)
        first, (piece, to) = self.sent[0], here

        @pl.when(self.alone)
        def _():
            to[...] = piece[...]

        @pl.when(jnp.logical_not(self.alone))
        def _():
            first.start()

    def wait_first(self):
        @pl.when(jnp.logical_not(self.alone))
        def _():
            self.sent[0].wait_send()

    def start(self):
        net = self.net
        for w in range(8):
            slot = self.data.at[net.z, net.x, w // 2, pl.ds(16 * (w % 2), 16)]
            copy = net.make(slot, slot, net.at(c=1 - net.c), self.base + w)

            @pl.when(jnp.logical_not(jnp.logical_and(self.alone, self.w == w)))
            def _():
                copy.wait_recv()

        self.plane.start(*ORDER)

    def unpack(self, out):
        data = self.data

        def body(y, _):
            for c in (0, 1):
                for half in (0, 1):
                    parts = [
                        data[z, 2 * i + half, y, 16 * c : 16 * c + 16]
                        for z in range(4)
                        for i in (0, 1)
                    ]
                    at = pl.multiple_of(y * 256 + c * 128, 128)
                    out[pl.ds(at, 128), 256 * half : 256 * half + 256] = jnp.concatenate(
                        parts, axis=0
                    )
            return 0

        lax.fori_loop(0, 4, body, 0)


def share_of(ref, z, x):
    return ref[z, x].reshape(128, 256)


def wide_of(ref, z):
    return jnp.concatenate([share_of(ref, z, x) for x in range(4)], axis=1)


def kernel(
    student_in,
    norm_gain,
    gate_weight,
    up_weight,
    down_weight,
    projection,
    teacher_in,
    teacher_gate,
    teacher_up,
    teacher_down,
    grad_gate,
    grad_up,
    grad_down,
    grad_proj,
    input_grad,
    xin,
    gain,
    wg,
    wu,
    wd,
    pj,
    tin,
    tg,
    tu,
    td,
    tdt,
    parts,
    mate,
    ring,
    thid,
    feat,
    feat1,
    featm,
    feat2,
    sums,
    sums1,
    summ,
    sums2,
    normed,
    summed,
    bgrad,
    ncols,
    scols,
    bcols,
    flat,
    nflat,
    hids,
    errs,
    ggs,
    gate,
    upsum,
    sigma,
    acc,
    acc2,
    tshare,
    target,
    fgrad,
    stat,
    statx,
    statz,
    invs,
    ogg,
    ogu,
    ogd,
    ogp,
    oig,
    load,
    store,
    send,
    recv,
):
    net = Net(send, recv)
    z, x, y, c = net.z, net.x, net.y, net.c
    ys = [mod4(y + o) for o in range(4)]

    rows_in = [pl.ds(pl.multiple_of(d * 256, 256), 256) for d in ys]
    loads = {}
    for i, (name, src, dst) in enumerate(
        (
            (2, teacher_in.at[rows_in[2]], tin.at[rows_in[2]]),
            ("tg", teacher_gate, tg),
            ("tu", teacher_up, tu),
            (1, teacher_in.at[rows_in[1]], tin.at[rows_in[1]]),
            (3, teacher_in.at[rows_in[3]], tin.at[rows_in[3]]),
            (0, teacher_in.at[rows_in[0]], tin.at[rows_in[0]]),
            ("xin", student_in, xin),
            ("gain", norm_gain, gain),
            ("wg", gate_weight, wg),
            ("wu", up_weight, wu),
            ("wd", down_weight, wd),
            ("td", teacher_down, td),
            ("pj", projection, pj),
        )
    ):
        loads[name] = pltpu.make_async_copy(src, dst, load.at[i])
        loads[name].start()

    barrier = pltpu.get_barrier_semaphore()
    peers = [net.at(y=mod4(y + o), c=lax.rem(c + f, 2)) for o in range(4) for f in (0, 1) if o or f]
    peers += [net.along("x", o) for o in (1, 2, 3)] + [net.along("z", o) for o in (1, 2, 3)]
    for peer in peers:
        pl.semaphore_signal(barrier, inc=1, device_id=peer, device_id_type=MESH)
    near = 2 * c + lax.rem(x, 2)
    for o in range(4):
        for f in (0, 1):
            source = net.at(z=y, x=near, y=mod4(y + o), c=lax.rem(c + f, 2))
            if o or f:
                pl.semaphore_signal(barrier, inc=1, device_id=source, device_id_type=MESH)
            else:

                @pl.when(jnp.logical_or(z != y, x != near))
                def _():
                    pl.semaphore_signal(barrier, inc=1, device_id=source, device_id_type=MESH)

    tsum = RingSum(
        net, "y", lambda d, h: parts.at[d, c, pl.ds(64 * h, 64)], ring
    )
    pair = {}

    def project(o):
        d = ys[o]
        loads[o].wait()
        rows = tin[rows_in[o], :]
        if o == 2:
            loads["tg"].wait()
        parts[d, :, :, 0:896] = mm(rows, tg[...], NN).astype(BF16).reshape(2, 128, 896)
        if o == 2:
            loads["tu"].wait()
        parts[d, :, :, 896:1792] = mm(rows, tu[...], NN).astype(BF16).reshape(2, 128, 896)

    def swap(o):
        d = ys[o]
        pair[o] = net.put(parts.at[d, 1 - c], mate.at[d], net.at(c=1 - c))

    def join(o):
        d = ys[o]
        pair[o].wait_recv()
        parts[d, c] = (up(parts[d, c]) + up(mate[d])).astype(BF16)

    project(2)
    own = jnp.logical_and(y == z, c == lax.div(x, 2)).astype(jnp.int32)
    pl.semaphore_wait(barrier, len(peers) + 8 - own)
    swap(2)
    project(1)
    swap(1)
    join(2)
    tsum.far()
    project(3)
    swap(3)
    join(1)
    tsum.near_r()

    loads["xin"].wait()
    loads["gain"].wait()

    def squares(b, total):
        v = up(xin[:, pl.ds(pl.multiple_of(b * 256, 256), 256)])
        return total + v * v

    total = lax.fori_loop(0, 16, squares, jnp.zeros((128, 256), F32))
    inv = lax.rsqrt(jnp.sum(total, axis=1, keepdims=True) / 4096.0 + 1e-05)
    invs[...] = jnp.broadcast_to(inv, (128, 128))

    def norm(b, _):
        at = pl.ds(pl.multiple_of(b * 256, 256), 256)
        scale = jnp.concatenate([invs[...], invs[...]], axis=1)
        v = up(xin[:, at]) * scale * gain[:, at]
        normed[lax.div(b, 4), lax.rem(b, 4)] = v.astype(BF16).reshape(4, 32, 256)
        return 0

    lax.fori_loop(0, 16, norm, 0)

    for name in ("wg", "wu", "wd"):
        loads[name].wait()

    def students(first, second, source, out_first, out_second):
        def body(b, _):
            at = pl.ds(pl.multiple_of(b * 1024, 1024), 1024)
            wide = wide_of(source, b)
            out_first[...] += mm(first[:, at], wide, NT)
            if second is not None:
                out_second[...] += mm(second[:, at], wide, NT)
            return 0

        out_first[...] = jnp.zeros(out_first.shape, F32)
        if second is not None:
            out_second[...] = jnp.zeros(out_second.shape, F32)
        lax.fori_loop(0, 4, body, 0)

    def back(out, pairs):
        def body(b, _):
            at = pl.ds(pl.multiple_of(b * 1024, 1024), 1024)
            v = sum(mm(small, w[:, at], TN) for small, w in pairs).astype(BF16)
            for i in range(4):
                out[b, i] = v[:, 256 * i : 256 * i + 256].reshape(4, 32, 256)
            return 0

        lax.fori_loop(0, 4, body, 0)

    def plane_sums(n):
        data = sums.at[n]

        def block(q):
            if q < 2:
                axes, src = ("x", "z"), lambda d: data.at[:, d, q]
            else:
                axes, src = ("z", "x"), lambda d: data.at[d, :, q]
            return PlaneSum(net, axes, src, sums1.at[n, q], summ.at[n, q], sums2.at[n, q])

        return [block(q) for q in range(4)]

    students(wg, wu, normed, gate, upsum)
    join(3)
    tsum.near_l()
    sig = jax.nn.sigmoid(gate[...])
    sigma[...] = sig
    hid = (gate[...] * sig * upsum[...]).astype(BF16)
    hiddens = TokenDirect(net, hids)
    hiddens.own[...] = hid
    back(sums.at[0], ((hid, wd),))
    branch = plane_sums(0)
    for q in ORDER:
        branch[q].start()
    tsum.relay()
    project(0)
    swap(0)
    loads["td"].wait()
    tdt[...] = td[...].T
    join(0)
    for q in ORDER:
        branch[q].turn()

    first, second = tsum.finish()
    sums_all = jnp.concatenate([first, second], axis=0)
    g = sums_all[:, :896]
    teach = g * jax.nn.sigmoid(g) * sums_all[:, 896:]
    teachers = TokenAll(net, thid)
    teachers.own[...] = teach.T.astype(BF16)
    teachers.start()

    order = [ys[0], ys[1], ys[3], ys[2]]

    def group(k):
        d = order[k]
        if k % 2 == 0:
            axes, src = ("x", "z"), lambda e: feat.at[:, e, d]
        else:
            axes, src = ("z", "x"), lambda e: feat.at[e, :, d]
        return PlaneSum(net, axes, src, feat1.at[k], featm.at[k], feat2.at[k])

    teaching = [group(k) for k in range(4)]

    def feature(k, o):
        d = ys[o]
        teachers.wait(o)
        v = mm(tdt[...], thid[:, pl.ds(pl.multiple_of(d * 256, 256), 256)], NN).astype(BF16)
        for f in (0, 1):
            feat[:, :, d, 64 * f : 64 * f + 64] = v[:, 128 * f : 128 * f + 128].reshape(
                4, 4, 64, 128
            )
        teaching[k].start()

    rows_of = lambda q: pl.ds(32 * q, 32)
    share_at = pl.ds(pl.multiple_of((z * 4 + x) * 256, 256), 256)
    sizes = (sums2.at[0, 0], sums1.at[0, 0])
    sum_all = PlaneAll(net, summed, sizes)
    for q in ORDER:
        v = branch[q].finish()
        summed[z, x, q] = (up(xin[rows_of(q), share_at]) + v).astype(BF16)
        sum_all.start(q)
    feature(0, 0)
    teachers.relay()
    sum_all.ring_turn()
    teachers.near()
    feature(1, 1)
    teachers.finish()
    feature(2, 3)
    teaching[0].turn()
    feature(3, 2)
    sum_all.ring_relay()
    ncol = Direct(net, normed, ncols)
    ncol.start((2, 1, 3, 0))
    sent = net.group(target.at[pl.ds(0, 448)])

    def hand(k, v):
        d = order[k]
        tshare[d] = v.astype(BF16)
        to = target.at[pl.ds(pl.multiple_of((y * 2 + c) * 64, 64), 64)]
        for f in (0, 1):
            cc = lax.rem(c + f, 2)
            piece = tshare.at[d, pl.ds(pl.multiple_of(cc * 64, 64), 64)]
            if k == 0 and f == 0:
                to[...] = piece[...]
            else:
                sent.put(piece, to, net.at(y=d, c=cc))

    teaching[1].turn()
    teaching[2].turn()
    teaching[3].turn()
    sum_all.ring_finish()
    loads["pj"].wait()
    students(pj, None, summed, acc, None)
    for k in range(4):
        hand(k, teaching[k].finish())
    sent.wait_recv()

    err = ((acc[...] - up(target[...])) * (1.0 / 32.0)).astype(BF16)
    errors = TokenDirect(net, errs)
    errors.own[...] = err
    errors.start()
    back(sums.at[1], ((err, pj),))
    grads = plane_sums(1)
    for q in ORDER:
        grads[q].start()
    scol = Direct(net, summed, scols)
    scol.start((2, 0))
    for q in ORDER:
        grads[q].turn()
    grad_all = PlaneAll(net, bgrad, sizes)
    for q in ORDER:
        v = grads[q].finish()
        bgrad[z, x, q] = v.astype(BF16)
        grad_all.start(q)
        fgrad[rows_of(q), :] = v
    bcol = Columns(net, bgrad, bcols, sizes)
    bcol.spread()
    grad_all.turn(0, 2)
    errors.pass_on()
    scol.start((1, 3))
    hiddens.start()
    grad_all.turn(1, 3)
    errors.finish()
    bcol.start()
    grad_all.finish()

    students(wd, None, bgrad, acc2, None)
    hg = acc2[...]
    g, s = gate[...], sigma[...]
    gg = (hg * upsum[...] * s * (1.0 + g * (1.0 - s))).astype(BF16)
    ug = (hg * g * s).astype(BF16)
    moment = jnp.sum(up(gg) * g + up(ug) * upsum[...], axis=0, keepdims=True)
    gates = [TokenDirect(net, ggs.at[pl.ds(448 * i, 448)]) for i in (0, 1)]
    own_at = pl.ds(pl.multiple_of((y * 2 + c) * 128, 128), 128)
    ggs[0:448, own_at] = gg
    ggs[448:896, own_at] = ug
    gates[0].start()
    gates[1].start()

    def tell(ref, me, axis):
        group = net.group(ref.at[pl.ds(0, 3)])
        for o in (2, 1, 3):
            group.put(ref.at[me], ref.at[me], net.along(axis, o))
        return group

    statx[x] = jnp.broadcast_to(moment, (8, 128))
    stats = tell(statx, x, "x")
    bcol.plane.turn(0, 2)
    back(sums.at[2], ((gg, wg), (ug, wu)))
    inner = plane_sums(2)
    for q in ORDER:
        inner[q].start()
    bcol.plane.turn(1, 3)
    stats.wait_recv()
    statz[z] = statx[0] + statx[1] + statx[2] + statx[3]
    stats = tell(statz, z, "z")
    hiddens.pass_on()
    scol.unpack(flat)

    outs = []

    def write(i, src, dst):
        outs.append(pltpu.make_async_copy(src, dst, store.at[i]))
        outs[-1].start()

    ogp[...] = mm(errs[...], flat[...], NN).astype(BF16)
    write(0, ogp, grad_proj)
    ncol.unpack(nflat)
    gates[0].pass_on()
    for q in ORDER:
        inner[q].turn()
    gates[0].finish()
    ogg[...] = mm(ggs[0:448], nflat[...], NN).astype(BF16)
    write(2, ogg, grad_gate)
    gates[1].pass_on()
    gates[1].finish()
    ogu[...] = mm(ggs[448:896], nflat[...], NN).astype(BF16)
    write(3, ogu, grad_up)
    bcol.plane.finish()
    bcol.unpack(flat)
    hiddens.finish()
    ogd[...] = mm(hids[...], flat[...], NN).astype(BF16)
    write(4, ogd, grad_down)
    stats.wait_recv()
    whole = (statz[0] + statz[1] + statz[2] + statz[3]) / 4096.0
    stat[...] = jnp.broadcast_to(whole[0:1], (128, 128)).T
    for q in ORDER:
        v = inner[q].finish()
        r = rows_of(q)
        scale = jnp.concatenate([invs[r, :], invs[r, :]], axis=1)
        mean = jnp.concatenate([stat[r, :], stat[r, :]], axis=1)
        scaled = v * gain[:, share_at]
        oig[r, :] = fgrad[r, :] + scale * (scaled - up(xin[r, share_at]) * scale * mean)
    write(1, oig, input_grad)
    bcol.wait_first()
    for copy in net.copies:
        copy.wait_send()
    for copy in outs:
        copy.wait()


def move(*refs):
    srcs, dsts, held = refs[0:5], refs[5:10], refs[10:15]
    came, went = refs[15], refs[16]
    ins, outs = [], []
    for part in range(4):
        for s, h, d in zip(srcs, held, dsts):
            rows = pl.ds(part * (s.shape[0] // 4), s.shape[0] // 4)
            i = len(ins)
            ins.append(pltpu.make_async_copy(s.at[rows], h.at[rows], came.at[i]))
            outs.append(pltpu.make_async_copy(h.at[rows], d.at[rows], went.at[i]))
    for copy in ins:
        copy.start()
    for i, copy in zip(ins, outs):
        i.wait()
        copy.start()
    for copy in outs:
        copy.wait()


def shards(
    student_in,
    norm_gain,
    gate_weight,
    up_weight,
    down_weight,
    projection,
    teacher_in,
    teacher_gate,
    teacher_up,
    teacher_down,
):
    vmem = pltpu.VMEM
    anyspec = pl.BlockSpec(memory_space=pl.ANY)
    shapes = (
        jax.ShapeDtypeStruct((448, 512), BF16),
        jax.ShapeDtypeStruct((448, 512), BF16),
        jax.ShapeDtypeStruct((448, 512), BF16),
        jax.ShapeDtypeStruct((512, 512), BF16),
        jax.ShapeDtypeStruct((128, 256), F32),
    )
    made = pl.pallas_call(
        kernel,
        out_shape=shapes,
        in_specs=[anyspec] * 10,
        out_specs=(anyspec,) * 5,
        scratch_shapes=[
            vmem((128, 4096), BF16),
            vmem((1, 4096), F32),
            vmem((448, 4096), BF16),
            vmem((448, 4096), BF16),
            vmem((448, 4096), BF16),
            vmem((512, 4096), BF16),
            vmem((1024, 1024), BF16),
            vmem((1024, 896), BF16),
            vmem((1024, 896), BF16),
            vmem((896, 1024), BF16),
            vmem((1024, 896), BF16),
            vmem((4, 2, 128, 1792), BF16),
            vmem((4, 128, 1792), BF16),
            vmem((6, 64, 1792), BF16),
            vmem((896, 1024), BF16),
            vmem((4, 4, 4, 128, 128), BF16),
            vmem((4, 3, 4, 128, 128), BF16),
            vmem((4, 4, 128, 128), BF16),
            vmem((4, 3, 128, 128), BF16),
            vmem((3, 4, 4, 4, 32, 256), BF16),
            vmem((3, 4, 3, 4, 32, 256), BF16),
            vmem((3, 4, 4, 32, 256), BF16),
            vmem((3, 4, 3, 32, 256), BF16),
            vmem((4, 4, 4, 32, 256), BF16),
            vmem((4, 4, 4, 32, 256), BF16),
            vmem((4, 4, 4, 32, 256), BF16),
            vmem((8, 2, 4, 32, 256), BF16),
            vmem((8, 2, 4, 32, 256), BF16),
            vmem((4, 4, 4, 32, 256), BF16),
            vmem((1024, 512), BF16),
            vmem((1024, 512), BF16),
            vmem((448, 1024), BF16),
            vmem((512, 1024), BF16),
            vmem((896, 1024), BF16),
            vmem((448, 128), F32),
            vmem((448, 128), F32),
            vmem((448, 128), F32),
            vmem((512, 128), F32),
            vmem((448, 128), F32),
            vmem((4, 128, 128), BF16),
            vmem((512, 128), BF16),
            vmem((128, 256), F32),
            vmem((128, 128), F32),
            vmem((4, 8, 128), F32),
            vmem((4, 8, 128), F32),
            vmem((128, 128), F32),
            vmem((448, 512), BF16),
            vmem((448, 512), BF16),
            vmem((448, 512), BF16),
            vmem((512, 512), BF16),
            vmem((128, 256), F32),
            pltpu.SemaphoreType.DMA((13,)),
            pltpu.SemaphoreType.DMA((5,)),
            pltpu.SemaphoreType.DMA((SEMS,)),
            pltpu.SemaphoreType.DMA((SEMS,)),
        ],
        compiler_params=pltpu.CompilerParams(
            collective_id=0, has_side_effects=True, vmem_limit_bytes=67043328
        ),
    )(
        student_in,
        norm_gain.reshape(1, -1),
        gate_weight.T,
        up_weight.T,
        down_weight,
        projection.transpose(1, 2, 0).reshape(512, -1),
        teacher_in,
        teacher_gate,
        teacher_up,
        teacher_down,
    )
    gg, gu, gd, gp, ig = pl.pallas_call(
        move,
        out_shape=shapes,
        in_specs=[anyspec] * 5,
        out_specs=(anyspec,) * 5,
        scratch_shapes=[vmem(s.shape, s.dtype) for s in shapes]
        + [pltpu.SemaphoreType.DMA((20,)), pltpu.SemaphoreType.DMA((20,))],
    )(*made)
    return gg.T, gu.T, gd, gp.reshape(8, 64, 512).transpose(2, 0, 1), ig


def solution(mesh):
    split = Mesh(mesh.devices.reshape(2, 4, 2, 2, 4), ("zh", "y", "c", "zl", "x"))
    in_specs = (
        P(WID, None),
        P(),
        P(None, GH),
        P(None, GH),
        P(GH, None),
        P(None, None, GH),
        P(None, WID),
        P(WID, GH),
        P(WID, GH),
        P(GH, WID),
    )
    out_specs = (
        P(WID, GH),
        P(WID, GH),
        P(GH, WID),
        P(WID, None, GH),
        P(WID, GH),
    )
    return jax.shard_map(
        shards, mesh=split, in_specs=in_specs, out_specs=out_specs, check_vma=False
    )
```
